512 devices in a mesh: dp: 64 (over x_lo, z, core), ctx: 8 (over x_hi, y).
Axes of the slice: x: 4 (x_hi: 2, x_lo: 2; x = x_hi * 2 + x_lo), y: 4, z: 16, core: 2. Of those that a mesh axis runs over, the one named last changes fastest.
Arguments:
- query_vecs: bfloat16 [64, 1024, 1024], P('dp', 'ctx'), may hold values from -12 to 12, as said below
- key_vecs: bfloat16 [64, 1024, 1024], P('dp', 'ctx'), may hold values from -12 to 12
- value_vecs: bfloat16 [64, 1024, 1024], P('dp', 'ctx'), may hold values from -6 to 6
- residual: bfloat16 [64, 1024, 2048], P('dp', 'ctx'), may hold values from -45 to 45
- w_out: bfloat16 [1024, 2048], P('dp'), may hold values from -0.75 to 0.75
- norm_gain: float32 [2048], replicated, may hold values from 0.25 to 1.75
- w_gate_up: bfloat16 [64, 2, 2048, 1408], P('dp', None, None, 'ctx'), may hold values from -0.125 to 0.125
- w_down: bfloat16 [64, 1408, 2048], P('dp', 'ctx'), may hold values from -0.15625 to 0.15625
- expert_ids: int32 [64, 1024, 6], P('dp', 'ctx'), may hold values from 0 to 63, as said below
- route_gates: float32 [64, 1024, 6], P('dp', 'ctx'), may hold values from 0.1 to 0.9
- capacity: int32 [64, 8, 2], P('dp', 'ctx'), may hold values from 12 to 24, as said below
- expert_owner: int32 [64], replicated, may hold values from 0 to 63, each once
Outputs:
- attn_proj: bfloat16 [64, 1024, 2048], P('dp', 'ctx')
- expert_sum: bfloat16 [64, 1024, 2048], P('dp', 'ctx')
The draws below stay inside these ranges and needn't reach their ends.
Inputs may be any that keep to these rules, and one draw needn't show every extreme that they name: `query_vecs`: q and k are drawn together. `expert_ids`: each position names 6 different experts; in each aligned block of 128 positions, experts 0 to 1 are each named by at least 24 positions. In each block some expert has capacity 24. `expert_owner`: each index of dp holds one expert.
All inputs are finite; a program needn't handle non-finite values.
Results may differ from the reference program's by a relative error of at most 0.019.
Values may be sent and summed in bfloat16 or wider, within the bound.
A program may use at most 64 MiB of HBM per device.

```python
import jax
import jax.numpy as jnp
from jax import lax

D = 2048
HEADS = 8
HD = 128
FF = 1408
PICKS_PER_TOKEN = 6
PASS_SPECIALISTS = 2
TOK_DEV = 128
SPECIALIST_TOTAL = 64
CAP = 24
TOKEN_SPAN = 1024
TEXT_COUNT = 64


def attention_pair(key):
    base = jax.random.fold_in(key, 4101)
    query_seed, key_seed = jax.random.split(base, 2)
    shape = (TEXT_COUNT, TOKEN_SPAN, HEADS, HD)
    queries = 1.3 * jnp.clip(jax.random.normal(query_seed, shape, jnp.float32), -5.0, 5.0)
    keys_out = jnp.clip(jax.random.normal(key_seed, shape, jnp.float32), -5.0, 5.0)
    return (queries.reshape(TEXT_COUNT, TOKEN_SPAN, HEADS * HD), keys_out.reshape(TEXT_COUNT, TOKEN_SPAN, HEADS * HD))


def draw_query_vecs(key, part):
    return attention_pair(key)[0].astype(jnp.bfloat16)


def draw_key_vecs(key, part):
    return attention_pair(key)[1].astype(jnp.bfloat16)


def draw_residual(key, part):
    base = jax.random.fold_in(key, 5303)
    noise_seed, row_seed, column_seed = jax.random.split(base, 3)
    shape = (TEXT_COUNT, TOKEN_SPAN, D)
    row_scale = jnp.exp(jax.random.uniform(row_seed, (TEXT_COUNT, TOKEN_SPAN, 1), jnp.float32, jnp.log(0.3), jnp.log(3.0)))
    column_scale = jnp.exp(jax.random.uniform(column_seed, (1, 1, D), jnp.float32, jnp.log(0.3), jnp.log(3.0)))
    values = jnp.clip(jax.random.normal(noise_seed, shape, jnp.float32), -5.0, 5.0) * row_scale * column_scale
    return values.astype(jnp.bfloat16)


def draw_expert_ids(key, part):
    base = jax.random.fold_in(key, 7207)
    score_seed, coin_seed, order_seed = jax.random.split(base, 3)
    gating_logits = jax.random.randint(score_seed, (TEXT_COUNT, TOKEN_SPAN, SPECIALIST_TOTAL), 0, 2 ** 20) * SPECIALIST_TOTAL + jnp.arange(SPECIALIST_TOTAL, dtype=jnp.int32)
    coins = jax.random.randint(coin_seed, (TEXT_COUNT, TOKEN_SPAN, PASS_SPECIALISTS), 0, 2)
    blocks = TEXT_COUNT * TOKEN_SPAN // TOK_DEV
    order = jax.random.randint(order_seed, (blocks, PASS_SPECIALISTS, TOK_DEV), 0, 2 ** 16) * TOK_DEV + jnp.arange(TOK_DEV, dtype=jnp.int32)
    places = jnp.argsort(jnp.argsort(order, axis=-1), axis=-1)
    forced = jnp.transpose(places < CAP, (0, 2, 1)).reshape(TEXT_COUNT, TOKEN_SPAN, PASS_SPECIALISTS)
    popular_specialists = (forced | (coins == 1)).astype(jnp.int32)
    added_preference = jnp.concatenate([popular_specialists * 2 ** 30, jnp.zeros((TEXT_COUNT, TOKEN_SPAN, SPECIALIST_TOTAL - PASS_SPECIALISTS), jnp.int32)], axis=-1)
    ignored_specialists, selected_specialists = lax.top_k(gating_logits + added_preference, PICKS_PER_TOKEN)
    return selected_specialists.astype(jnp.int32)


def draw_capacity(key, part):
    block_count = TOKEN_SPAN // TOK_DEV
    values = jax.random.randint(jax.random.fold_in(key, 9001), (TEXT_COUNT, block_count, PASS_SPECIALISTS), CAP // 2, CAP + 1)
    fullest = jax.random.randint(jax.random.fold_in(key, 9002), (TEXT_COUNT, block_count, 1), 0, PASS_SPECIALISTS)
    return jnp.where(jnp.arange(PASS_SPECIALISTS)[None, None, :] == fullest, CAP, values).astype(jnp.int32)


def block_levels(key, extent, cuts, least, high):
    loudness = 1.0
    for dim, blocks in cuts:
        steps = jax.random.uniform(jax.random.fold_in(jax.random.fold_in(key, 6), dim), (blocks,), jnp.float32, least / len(cuts), high / len(cuts))
        loudness = loudness * jnp.repeat(jnp.exp(steps), extent[dim] // blocks).reshape((-1,) + (1,) * (len(extent) - 1 - dim))
    return loudness


def centred(own_key, shape, width, limit, cuts=(), held_as=jnp.bfloat16):
    loudness = block_levels(own_key, shape, cuts, -0.22, 0.18) if cuts else 1.0
    result = jax.random.normal(own_key, shape, jnp.float32) * width * loudness
    return jnp.minimum(jnp.maximum(result, -limit), limit).astype(held_as)


def setup_inputs(seed: int = 0) -> dict:
    keys = jax.random.split(jax.random.key(seed), 13)
    query_vecs = draw_query_vecs(jax.random.fold_in(keys[12], 71), 0)
    key_vecs = draw_key_vecs(jax.random.fold_in(keys[12], 71), 0)
    value_vecs = centred(keys[2], (TEXT_COUNT, TOKEN_SPAN, HEADS * HD), 1.0, 6.0, ((0, 64), (1, 8)))
    residual = draw_residual(jax.random.fold_in(keys[12], 71), 0)
    w_out = centred(keys[4], (HEADS * HD, D), (HEADS * HD // 16) ** -0.5, 0.75, ((0, 64),))
    norm_gain = jnp.clip(1.0 + 0.15 * jax.random.normal(keys[5], (D,), jnp.float32), 0.25, 1.75)
    w_gate_up = centred(keys[6], (SPECIALIST_TOTAL, 2, D, FF), D ** -0.5, 0.125, ((0, 64), (3, 8)))
    w_down = centred(keys[7], (SPECIALIST_TOTAL, FF, D), FF ** -0.5, 0.15625, ((0, 64), (1, 8)))
    expert_ids = draw_expert_ids(jax.random.fold_in(keys[12], 71), 0)
    route_gates = jnp.clip(0.1 + 0.79999997 * jax.random.uniform(keys[9], (TEXT_COUNT, TOKEN_SPAN, PICKS_PER_TOKEN), jnp.float32) ** block_levels(keys[9], (TEXT_COUNT, TOKEN_SPAN, PICKS_PER_TOKEN), ((0, 64), (1, 8)), -0.2, 0.2), 0.1, 0.9)
    capacity = draw_capacity(jax.random.fold_in(keys[12], 71), 0)
    expert_owner = jax.random.permutation(keys[11], SPECIALIST_TOTAL).astype(jnp.int32)
    return dict(query_vecs=query_vecs, key_vecs=key_vecs, value_vecs=value_vecs, residual=residual, w_out=w_out, norm_gain=norm_gain, w_gate_up=w_gate_up, w_down=w_down, expert_ids=expert_ids, route_gates=route_gates, capacity=capacity, expert_owner=expert_owner)


EPSILON = 1e-06

def route_slots(expert_ids, route_gates, capacity, expert):
    matches = expert_ids == expert
    routed = jnp.any(matches, axis=1)
    gate_value = lax.optimization_barrier(jnp.sum(jnp.where(matches, route_gates, 0.0), axis=1))
    slot_rank = (jnp.cumsum(routed.astype(jnp.int32)) - 1).astype(jnp.int32)
    kept_mask = routed & (slot_rank < capacity[expert])
    return (slot_rank, kept_mask, gate_value)

def sequence_attention(tensors):
    query_part = tensors[0].astype(jnp.float32).reshape(TOKEN_SPAN, HEADS, HD)
    key_part = tensors[1].astype(jnp.float32).reshape(TOKEN_SPAN, HEADS, HD)
    value_part = tensors[2].astype(jnp.float32).reshape(TOKEN_SPAN, HEADS, HD)
    gating_logits = jnp.einsum('qhd,khd->hqk', query_part, key_part, precision=lax.Precision.HIGHEST) * HD ** (-0.5)
    position = jnp.arange(TOKEN_SPAN)
    visible = position[None, :] <= position[:, None]
    gating_logits = jnp.where(visible[None], gating_logits, -jnp.inf)
    row_top = lax.optimization_barrier(jnp.max(gating_logits, axis=-1, keepdims=True))
    weights = jnp.exp(gating_logits - row_top)
    row_total = lax.optimization_barrier(jnp.sum(weights, axis=-1))
    rounded = lax.optimization_barrier(weights.astype(jnp.bfloat16)).astype(jnp.float32)
    mixed = jnp.einsum('hqk,khd->qhd', rounded, value_part, precision=lax.Precision.HIGHEST)
    mixed = mixed / jnp.transpose(row_total)[:, :, None]
    return mixed.reshape(TOKEN_SPAN, HEADS * HD).astype(jnp.bfloat16)

def reference(query_vecs, key_vecs, value_vecs, residual, w_out, norm_gain, w_gate_up, w_down, expert_ids, route_gates, capacity, expert_owner):
    attended = lax.map(sequence_attention, (query_vecs, key_vecs, value_vecs))
    attn_proj = jnp.dot(attended.reshape(TEXT_COUNT * TOKEN_SPAN, HEADS * HD), w_out, preferred_element_type=jnp.float32).astype(jnp.bfloat16)
    combined = residual.reshape(TEXT_COUNT * TOKEN_SPAN, D).astype(jnp.float32) + attn_proj.astype(jnp.float32)
    normed = (combined * lax.rsqrt(lax.optimization_barrier(jnp.mean(combined * combined, axis=-1, keepdims=True)) + EPSILON) * norm_gain).astype(jnp.bfloat16)
    blocks = TEXT_COUNT * TOKEN_SPAN // TOK_DEV
    experts_in = [(w_gate_up[expert_owner[expert]], w_down[expert_owner[expert]]) for expert in range(PASS_SPECIALISTS)]
    slot_ids = jnp.arange(CAP)

    def block_output(tensors):
        normed_block, ids_block, gates_block, block_caps = tensors
        summed = jnp.zeros((TOK_DEV, D), jnp.float32)
        for expert in range(PASS_SPECIALISTS):
            slot_rank, kept_mask, gate_value = route_slots(ids_block, gates_block, block_caps, expert)
            select = ((slot_rank[None, :] == slot_ids[:, None]) & kept_mask[None, :]).astype(jnp.bfloat16)
            selected_specialists = jnp.dot(select, normed_block, preferred_element_type=jnp.float32).astype(jnp.bfloat16)
            gate_up, down_part = experts_in[expert]
            gate_proj = jnp.dot(selected_specialists, gate_up[0], preferred_element_type=jnp.float32)
            up_proj = jnp.dot(selected_specialists, gate_up[1], preferred_element_type=jnp.float32)
            hidden = (jax.nn.silu(gate_proj) * up_proj).astype(jnp.bfloat16)
            produced = jnp.dot(hidden, down_part, preferred_element_type=jnp.float32)
            picked = jnp.take(produced, jnp.clip(slot_rank, 0, CAP - 1), axis=0)
            summed = summed + jnp.where(kept_mask, gate_value, 0.0)[:, None] * picked
        return summed.astype(jnp.bfloat16)
    expert_sum = lax.map(block_output, (normed.reshape(blocks, TOK_DEV, D), expert_ids.reshape(blocks, TOK_DEV, PICKS_PER_TOKEN), route_gates.reshape(blocks, TOK_DEV, PICKS_PER_TOKEN), capacity.reshape(blocks, PASS_SPECIALISTS)))
    return (attn_proj.reshape(TEXT_COUNT, TOKEN_SPAN, D), expert_sum.reshape(TEXT_COUNT, TOKEN_SPAN, D))
```

```python
import functools

import jax
import jax.numpy as jnp
from jax import lax
from jax.experimental import pallas as pl
from jax.experimental.pallas import tpu as pltpu
from jax.sharding import PartitionSpec as P

D = 2048
HD = 128
FF_DEV = 176
CAP = 24
TOK = 128
NZ = 16
NY = 4
NX = 4
NCTX = 8
HALF = 272
HALF_STEP = 256
EPSILON = 1e-06
MESH = pl.DeviceIdType.MESH
BF = jnp.bfloat16
F32 = jnp.float32

NT = (((1,), (1,)), ((), ()))
TN = (((0,), (0,)), ((), ()))


def dot(a, b, dims=(((1,), (0,)), ((), ()))):
    return lax.dot_general(a, b, dims, preferred_element_type=F32)


def kernel(
    owner, caps,
    q_ref, k_ref, v_ref, res_ref, wo_ref, w_ref, gain_ref, ids_ref, gates_ref,
    proj_ref, sum_ref,
    qkv, abuf, attd, wbuf, res, own, oth, cand, rsb, xpiece, wf, uw,
    normed, rbuf, dsend, sbuf, pbuf, xo, xi,
    q_s, q_r, a_s, a_r, z_s, z_r, p1_s, p1_r, p2_s, p2_r, c_s, c_r,
    l_s, oth_s, oth_r, rs_s, rs_r, xp_s, xp_r, ag_s, ag_r, cc_s, cc_r,
    d_s, d_r, r_s, r_r, e_s, e_r, o_s, o_r,
):
    dp = lax.axis_index("dp")
    ctx = lax.axis_index("ctx")
    core = lax.rem(dp, 2)
    z = lax.rem(dp // 2, NZ)
    xl = dp // (2 * NZ)
    xh = ctx // NY
    y = lax.rem(ctx, NY)
    x = xh * 2 + xl

    def at(xx=None, yy=None, zz=None, cc=None):
        xx = x if xx is None else xx
        yy = y if yy is None else yy
        zz = z if zz is None else zz
        cc = core if cc is None else cc
        return ((lax.rem(xx, 2) * NZ + zz) * 2 + cc, (xx // 2) * NY + yy)

    partner = at(xx=x + 1 - 2 * xl)
    sibling = at(cc=1 - core)
    up = at(zz=lax.rem(z + 1, NZ))
    down = at(zz=lax.rem(z + NZ - 1, NZ))

    pending = []

    def send(src, dst, ssem, rsem, dev):
        copy = pltpu.make_async_remote_copy(
            src_ref=src, dst_ref=dst, send_sem=ssem, recv_sem=rsem,
            device_id=dev, device_id_type=MESH,
        )
        copy.start()
        pending.append(copy)

    def arrive(dst, sem):
        pltpu.make_async_copy(dst, dst, sem).wait()

    barrier = pltpu.get_barrier_semaphore()
    partners = [at(zz=lax.rem(z + i, NZ)) for i in range(1, NZ)]
    partners += [(dp, lax.rem(ctx + i, NCTX)) for i in range(1, NCTX)]
    partners += [partner, at(xx=lax.rem(x + 3 - 2 * xl, NX)), sibling]
    for dev in partners:
        pl.semaphore_signal(barrier, inc=1, device_id=dev, device_id_type=MESH)
    pl.semaphore_wait(barrier, len(partners))

    def cols(start, size):
        return pl.ds(pl.multiple_of(start, 128), size)

    half_rows = pl.ds(pl.multiple_of(core * HALF_STEP, 16), HALF)
    other_rows = pl.ds(pl.multiple_of((1 - core) * HALF_STEP, 16), HALF)
    send(w_ref.at[other_rows, :], oth, oth_s, oth_r, sibling)
    own_copy = pltpu.make_async_copy(w_ref.at[half_rows, :], own, l_s.at[0])
    own_copy.start()
    for i in range(1, NCTX):
        peer = lax.rem(ctx + i, NCTX)
        for j, ref in enumerate((q_ref, k_ref, v_ref)):
            send(ref.at[:, cols(peer * HD, HD)], qkv.at[j, ctx], q_s.at[j, i], q_r.at[j, ctx], (dp, peer))
    for j, ref in enumerate((q_ref, k_ref, v_ref)):
        pltpu.make_async_copy(ref.at[:, cols(ctx * HD, HD)], qkv.at[j, ctx], q_r.at[j, ctx]).start()
    for i in range(1, NZ):
        send(wo_ref.at[:, cols(ctx * 256, 256)], wbuf.at[x, y, z, core], z_s.at[i], z_r.at[z], at(zz=lax.rem(z + i, NZ)))
    pltpu.make_async_copy(wo_ref.at[:, cols(ctx * 256, 256)], wbuf.at[x, y, z, core], z_r.at[z]).start()
    res_copy = pltpu.make_async_copy(res_ref, res, l_s.at[1])
    res_copy.start()

    owner0 = owner[0]
    owner1 = owner[1]

    def weights():
        own_copy.wait()
        arrive(oth, oth_r)
        mate = dp + 1 - 2 * core
        has = []
        for e, root in enumerate((owner0, owner1)):
            mine = root == dp
            mates = root == mate
            has.append(jnp.logical_or(mine, mates))
            for c in range(NZ):
                a = own[:, c * 128:(c + 1) * 128]
                b = oth[:, c * 128:(c + 1) * 128]
                cand[e, c] = lax.select(mine, a, lax.select(mates, b, jnp.zeros_like(b)))
        to = (up, down)

        def chunk(d, t):
            return lax.rem(z + 2 * NZ - 2 - t, NZ) if d == 0 else lax.rem(z + 2 + t, NZ)

        for d in range(2):
            send(cand.at[d, chunk(d, -1)], rsb.at[d, 0], rs_s.at[d, 0], rs_r.at[d, 0], to[d])
        yield
        for t in range(NZ - 1):
            for d in range(2):
                arrive(rsb.at[d, t], rs_r.at[d, t])
                rsb[d, t] = lax.select(has[d], cand[d, chunk(d, t)], rsb[d, t])
                if t < NZ - 2:
                    send(rsb.at[d, t], rsb.at[d, t + 1], rs_s.at[d, t + 1], rs_r.at[d, t + 1], to[d])
            yield
        send(rsb.at[1 - xl, NZ - 2], xpiece, xp_s, xp_r, partner)
        yield
        arrive(xpiece, xp_r)
        root = jnp.where(xl == 0, owner0, owner1)
        there = (root // (2 * NZ)) != xl
        wf[core, :, cols(z * 128, 128)] = lax.select(there, xpiece[...], rsb[xl, NZ - 2])

        def piece(c):
            return wf.at[core, :, cols(c * 128, 128)]

        for d in range(2):
            send(piece(z), piece(z), ag_s.at[d, 0], ag_r.at[d, 0], to[d])
        send(piece(z), piece(z), cc_s.at[0], cc_r.at[z], sibling)
        yield
        for t in range(NZ // 2):
            for d in range(2):
                last = NZ // 2 - 1 - d
                if t > last:
                    continue
                c = lax.rem(z + NZ - 1 - t, NZ) if d == 0 else lax.rem(z + 1 + t, NZ)
                arrive(piece(c), ag_r.at[d, t])
                if t < last:
                    send(piece(c), piece(c), ag_s.at[d, t + 1], ag_r.at[d, t + 1], to[d])
                send(piece(c), piece(c), cc_s.at[1 + 2 * t + d], cc_r.at[c], sibling)
            yield

    def route(e):
        match = ids_ref[...] == e
        routed = jnp.sum(jnp.where(match, 1.0, 0.0), axis=1, keepdims=True)
        gate = jnp.sum(jnp.where(match, gates_ref[...], 0.0), axis=1, keepdims=True)
        rows = lax.broadcasted_iota(jnp.int32, (TOK, TOK), 0)
        lanes = lax.broadcasted_iota(jnp.int32, (TOK, TOK), 1)
        before = jnp.where(lanes < rows, 1.0, 0.0).astype(BF)
        wide = jnp.broadcast_to(routed, (TOK, TOK))
        rank = dot(before, wide.astype(BF))
        cap = jnp.where(e == 0, caps[0], caps[1]).astype(F32)
        kept = jnp.logical_and(wide > 0.5, rank < cap)
        slot = lanes.astype(F32)
        first = jnp.where(jnp.logical_and(kept, rank == slot), 1.0, 0.0)[:, : 2 * CAP]
        second = jnp.where(jnp.logical_and(kept, rank == slot - CAP), 1.0, 0.0)[:, : 2 * CAP]
        return first.astype(BF), second.astype(BF), gate

    def main():
        for i in range(NZ):
            arrive(wbuf.at[x, y, i, core], z_r.at[i])
        a_own = wbuf.at[x, y, pl.ds(0, 8), core]
        b_own = wbuf.at[x, y, pl.ds(8, 8), core]
        for i in range(1, 4):
            xx, yy = lax.rem(x + i, NX), lax.rem(y + i, NY)
            send(a_own, a_own, p1_s.at[0, i], p1_r.at[0, x], at(xx=xx))
            send(b_own, b_own, p1_s.at[1, i], p1_r.at[1, y], at(yy=yy))
        yield
        for i in range(1, 4):
            xx, yy = lax.rem(x + i, NX), lax.rem(y + i, NY)
            arrive(wbuf.at[xx, y, pl.ds(0, 8), core], p1_r.at[0, xx])
            arrive(wbuf.at[x, yy, pl.ds(8, 8), core], p1_r.at[1, yy])

        def a_slab(yy):
            return wbuf.at[:, yy, pl.ds(0, 8), core]

        def b_slab(xx):
            return wbuf.at[xx, :, pl.ds(8, 8), core]

        for i in range(1, 4):
            xx, yy = lax.rem(x + i, NX), lax.rem(y + i, NY)
            send(a_slab(y), a_slab(y), p2_s.at[0, i], p2_r.at[0, y], at(yy=yy))
            send(b_slab(x), b_slab(x), p2_s.at[1, i], p2_r.at[1, x], at(xx=xx))
        send(a_slab(y), a_slab(y), c_s.at[0, 0], c_r.at[0, y], sibling)
        send(b_slab(x), b_slab(x), c_s.at[1, 0], c_r.at[1, x], sibling)
        yield
        for b in range(4):
            for i in (2 * b, 2 * b + 1):
                for j in range(3):
                    arrive(qkv.at[j, i], q_r.at[j, i])
            n = (b + 1) * 256
            q = qkv[0, 2 * b:2 * b + 2].reshape(256, HD)
            k = qkv[1, : 2 * b + 2].reshape(n, HD)
            v = qkv[2, : 2 * b + 2].reshape(n, HD)
            s = dot(q, k, NT) * HD ** (-0.5)
            qpos = lax.broadcasted_iota(jnp.int32, (256, n), 0) + b * 256
            kpos = lax.broadcasted_iota(jnp.int32, (256, n), 1)
            s = jnp.where(kpos <= qpos, s, -jnp.inf)
            w = jnp.exp(s - jnp.max(s, axis=1, keepdims=True))
            total = jnp.sum(w, axis=1, keepdims=True)
            o = dot(w.astype(BF), v) / total
            abuf[2 * b:2 * b + 2] = o.astype(BF).reshape(2, 128, HD)
            yield
        mine = attd.at[:, cols(ctx * HD, HD)]
        for i in range(1, NCTX):
            peer = lax.rem(ctx + i, NCTX)
            send(abuf.at[peer], mine, a_s.at[i], a_r.at[ctx], (dp, peer))
        pltpu.make_async_copy(abuf.at[ctx], mine, a_r.at[ctx]).start()
        yield
        for i in range(1, 4):
            xx, yy = lax.rem(x + i, NX), lax.rem(y + i, NY)
            arrive(a_slab(yy), p2_r.at[0, yy])
            send(a_slab(yy), a_slab(yy), c_s.at[0, i], c_r.at[0, yy], sibling)
            arrive(b_slab(xx), p2_r.at[1, xx])
            send(b_slab(xx), b_slab(xx), c_s.at[1, i], c_r.at[1, xx], sibling)
            yield
        for i in range(NCTX):
            arrive(attd.at[:, i * HD:(i + 1) * HD], a_r.at[i])
        for i in range(4):
            arrive(wbuf.at[:, i, pl.ds(0, 8), 1 - core], c_r.at[0, i])
            arrive(wbuf.at[i, :, pl.ds(8, 8), 1 - core], c_r.at[1, i])
        res_copy.wait()
        squares = jnp.zeros((TOK, 1), F32)
        for i in range(NCTX):
            acc = dot(attd[:, :512], wbuf[(i // NY) * 2, i % NY].reshape(512, 256))
            acc += dot(attd[:, 512:], wbuf[(i // NY) * 2 + 1, i % NY].reshape(512, 256))
            out = acc.astype(BF)
            here = slice(i * 256, (i + 1) * 256)
            proj_ref[:, here] = out
            combined = res[:, here].astype(F32) + out.astype(F32)
            squares += jnp.sum(combined * combined, axis=1, keepdims=True)
            if i % 4 == 3:
                yield
        scale = lax.rsqrt(squares * (1.0 / D) + EPSILON)
        for i in range(NCTX):
            here = slice(i * 256, (i + 1) * 256)
            combined = res[:, here].astype(F32) + proj_ref[:, here].astype(F32)
            normed[:, here] = (combined * scale * gain_ref[:, here]).astype(BF)
        first, second, _ = route(1 - xl)
        dsend[...] = (dot(first, normed[:, :1024], TN) + dot(second, normed[:, 1024:], TN)).astype(BF)
        send(dsend, rbuf.at[ctx, xl], d_s, d_r, partner)
        first, second, _ = route(xl)
        rbuf[ctx, xl] = (dot(first, normed[:, :1024], TN) + dot(second, normed[:, 1024:], TN)).astype(BF)
        for i in range(1, NCTX):
            peer = lax.rem(ctx + i, NCTX)
            send(rbuf.at[ctx, xl], rbuf.at[ctx, xl], r_s.at[0, i], r_r.at[0, ctx], (dp, peer))
        yield
        arrive(rbuf.at[ctx, 1 - xl], d_r)
        for i in range(1, NCTX):
            peer = lax.rem(ctx + i, NCTX)
            send(rbuf.at[ctx, 1 - xl], rbuf.at[ctx, 1 - xl], r_s.at[1, i], r_r.at[1, ctx], (dp, peer))
        yield

    threads = {"w": weights(), "m": main()}
    alive = dict(threads)
    for step in SCHEDULE:
        if step in alive and next(alive[step], 0) == 0:
            del alive[step]
    for step in ("m", "w"):
        if step in alive:
            for _ in alive[step]:
                pass

    for c in range(NZ):
        arrive(wf.at[1 - core, :, c * 128:(c + 1) * 128], cc_r.at[c])
    uw[0:80] = wf[0, 176:256]
    uw[80:176] = wf[1, 0:96]
    for i in range(1, NCTX):
        peer = lax.rem(ctx + i, NCTX)
        arrive(rbuf.at[peer, xl], r_r.at[0, peer])
        arrive(rbuf.at[peer, 1 - xl], r_r.at[1, peer])
    for g in range(2):
        r = rbuf[4 * g:4 * g + 4].reshape(384, 1024)
        pair = []
        for w in (wf.at[0, 0:176], uw):
            left = dot(r, w[:, :1024], NT).reshape(8, 48, FF_DEV)
            right = dot(r, w[:, 1024:], NT).reshape(8, 48, FF_DEV)
            pair.append((left[:, :CAP] + right[:, CAP:]).reshape(8 * CAP, FF_DEV))
        gate_proj, up_proj = pair
        hidden = (gate_proj / (1.0 + jnp.exp(-gate_proj)) * up_proj).astype(BF)
        for h in range(2):
            out = dot(hidden, wf[1, 96:272, h * 1024:(h + 1) * 1024]).reshape(8, CAP, 1024)
            if h == 0:
                kept_left = out
        packed = jnp.concatenate([kept_left, out], axis=1).astype(BF)
        sbuf[4 * g:4 * g + 4] = packed.reshape(4, 2, 48, 1024)
    for i in range(1, NCTX):
        peer = lax.rem(ctx + i, NCTX)
        send(sbuf.at[peer], pbuf.at[ctx], e_s.at[i], e_r.at[ctx], (dp, peer))
    for i in range(1, NCTX):
        peer = lax.rem(ctx + i, NCTX)
        arrive(pbuf.at[peer], e_r.at[peer])

    def total_of(side):
        acc = sbuf[ctx, side].astype(F32)
        for i in range(1, NCTX):
            acc += pbuf[lax.rem(ctx + i, NCTX), side].astype(F32)
        return acc.astype(BF)

    xo[...] = total_of(1 - xl)
    send(xo, xi, o_s, o_r, partner)
    mine = total_of(xl)
    first, second, gate = route(xl)
    left = gate * dot(first, mine)
    right = gate * dot(second, mine)
    arrive(xi, o_r)
    theirs = xi[...]
    first, second, gate = route(1 - xl)
    sum_ref[:, :1024] = (left + gate * dot(first, theirs)).astype(BF)
    sum_ref[:, 1024:] = (right + gate * dot(second, theirs)).astype(BF)
    for copy in pending:
        copy.wait_send()


SCHEDULE = "wmwwmwwmwmwmwmwmwwmwmwmwmwwmwwmwwmwwmwwwwwww"


def body(
    query_vecs, key_vecs, value_vecs, residual, w_out, norm_gain, w_gate_up,
    w_down, expert_ids, route_gates, capacity, expert_owner,
):
    packed = jnp.concatenate(
        [w_gate_up[0, 0].T, w_gate_up[0, 1].T, w_down[0]], axis=0
    )
    hbm = pl.BlockSpec(memory_space=pl.ANY)
    vmem = pl.BlockSpec(memory_space=pltpu.VMEM)
    smem = pl.BlockSpec(memory_space=pltpu.SMEM)
    dma = pltpu.SemaphoreType.DMA
    out = jax.ShapeDtypeStruct((TOK, D), BF)
    rows = (2, 48, 1024)
    attn_proj, expert_sum = pl.pallas_call(
        kernel,
        out_shape=(out, out),
        in_specs=[smem, smem] + [hbm] * 6 + [vmem] * 3,
        out_specs=(vmem, vmem),
        scratch_shapes=[
            pltpu.VMEM((3, NCTX, TOK, HD), BF),
            pltpu.VMEM((NCTX, TOK, HD), BF),
            pltpu.VMEM((TOK, NCTX * HD), BF),
            pltpu.VMEM((NX, NY, NZ, 2, 16, 256), BF),
            pltpu.VMEM((TOK, D), BF),
            pltpu.VMEM((HALF, D), BF),
            pltpu.VMEM((HALF, D), BF),
            pltpu.VMEM((2, NZ, HALF, 128), BF),
            pltpu.VMEM((2, NZ - 1, HALF, 128), BF),
            pltpu.VMEM((HALF, 128), BF),
            pltpu.VMEM((2, HALF, D), BF),
            pltpu.VMEM((FF_DEV, D), BF),
            pltpu.VMEM((TOK, D), BF),
            pltpu.VMEM((NCTX,) + rows, BF),
            pltpu.VMEM(rows[1:], BF),
            pltpu.VMEM((NCTX,) + rows, BF),
            pltpu.VMEM((NCTX,) + rows, BF),
            pltpu.VMEM(rows[1:], BF),
            pltpu.VMEM(rows[1:], BF),
            dma((3, NCTX)), dma((3, NCTX)),
            dma((NCTX,)), dma((NCTX,)),
            dma((NZ,)), dma((NZ,)),
            dma((2, 4)), dma((2, 4)),
            dma((2, 4)), dma((2, 4)),
            dma((2, 4)), dma((2, 4)),
            dma((2,)), dma, dma,
            dma((2, NZ - 1)), dma((2, NZ - 1)),
            dma, dma,
            dma((2, 8)), dma((2, 8)),
            dma((NZ + 1,)), dma((NZ,)),
            dma, dma,
            dma((2, NCTX)), dma((2, NCTX)),
            dma((NCTX,)), dma((NCTX,)),
            dma, dma,
        ],
        compiler_params=pltpu.CompilerParams(
            collective_id=0, has_side_effects=True, vmem_limit_bytes=58 << 20
        ),
    )(
        expert_owner[:2], capacity[0, 0],
        query_vecs[0], key_vecs[0], value_vecs[0], residual[0], w_out, packed,
        norm_gain[None], expert_ids[0], route_gates[0],
    )
    return (attn_proj[None], expert_sum[None])


def solution(mesh):
    seq = P("dp", "ctx", None)
    placed = (
        seq, seq, seq, seq, P("dp", None), P(),
        P("dp", None, None, "ctx"), seq, seq, seq, seq, P(),
    )
    return jax.shard_map(
        body, mesh=mesh, in_specs=placed, out_specs=(seq, seq), check_vma=False
    )
```

```python
import jax
import jax.numpy as jnp
from jax import lax
from jax.experimental import pallas as pl
from jax.experimental.pallas import tpu as pltpu
from jax.sharding import PartitionSpec as P

D = 2048
HD = 128
FF_DEV = 176
CAP = 24
TOK = 128
PICKS = 6
NZ = 16
NY = 4
NX = 4
NCTX = 8
HALF = 272
HALF_STEP = 256
HOPS = NZ // 2
EPSILON = 1e-06
MESH = pl.DeviceIdType.MESH
BF = jnp.bfloat16
F32 = jnp.float32

NN = (((1,), (0,)), ((), ()))
NT = (((1,), (1,)), ((), ()))
TN = (((0,), (0,)), ((), ()))

SCHEDULE = "wmwmwmmwmmmwwmwmmwmmwmwwwwwwwwww"
GROUPS = ((1, 2, 3, 4), (5, 6, 7, 0))
AG_PARTS = ((0, 144), (144, 128))


def dot(a, b, dims=NN):
    return lax.dot_general(a, b, dims, preferred_element_type=F32)


def cols(start, size):
    return pl.ds(pl.multiple_of(start, 128), size)


def slot_rows(ids_ref, cap, e):
    routed = jnp.zeros((1, TOK), F32)
    for i in range(PICKS):
        routed += jnp.where(ids_ref[i] == e, 1.0, 0.0)
    rows = lax.broadcasted_iota(jnp.int32, (TOK, TOK), 0)
    lanes = lax.broadcasted_iota(jnp.int32, (TOK, TOK), 1)
    before = jnp.where(rows < lanes, 1.0, 0.0).astype(BF)
    rank = dot(jnp.broadcast_to(routed, (8, TOK)).astype(BF), before)[0:1]
    kept = jnp.where(rank < cap.astype(F32), routed, 0.0)
    rank = jnp.where(kept > 0.5, rank, -1000.0)
    slot = lax.broadcasted_iota(jnp.int32, (2 * CAP, TOK), 0).astype(F32)
    first = jnp.where(rank == slot, 1.0, 0.0)
    second = jnp.where(rank == slot - CAP, 1.0, 0.0)
    return first, second


def kernel(
    owner, caps,
    q_ref, k_ref, v_ref, res_ref, wo_ref, wg_ref, wd_ref, gain_ref, ids_ref,
    proj_ref, tot_ref,
    qkv, abuf, attd, wbuf, res, packed, oth, cand, rsb, xsend, xpiece, wf, uw,
    normed, rbuf, dsend, sbuf, pbuf,
    q_s, q_r, a_s, a_r, z_s, z_r, p1_s, p1_r, p2_s, p2_r, c_s, c_r,
    l_s, oth_s, oth_r, rs_s, rs_r, xp_s, xp_r, ag_s, ag_r, cc_s, cc_r,
    r_s, r_r, e_s, e_r,
):
    dp = lax.axis_index("dp")
    ctx = lax.axis_index("ctx")
    core = lax.rem(dp, 2)
    z = lax.rem(dp // 2, NZ)
    xl = dp // (2 * NZ)
    xh = ctx // NY
    y = lax.rem(ctx, NY)
    x = xh * 2 + xl

    def at(xx=None, yy=None, zz=None, cc=None):
        xx = x if xx is None else xx
        yy = y if yy is None else yy
        zz = z if zz is None else zz
        cc = core if cc is None else cc
        return ((lax.rem(xx, 2) * NZ + zz) * 2 + cc, (xx // 2) * NY + yy)

    line = dp + 2 * NZ * (1 - 2 * xl)
    partner = (line, ctx)
    sibling = at(cc=1 - core)
    up = at(zz=lax.rem(z + 1, NZ))
    down = at(zz=lax.rem(z + NZ - 1, NZ))

    def peer(i):
        return lax.rem(ctx + i, NCTX)

    def send(src, dst, ssem, rsem, dev):
        pltpu.make_async_remote_copy(
            src_ref=src, dst_ref=dst, send_sem=ssem, recv_sem=rsem,
            device_id=dev, device_id_type=MESH,
        ).start()

    def local(src, dst, sem):
        pltpu.make_async_copy(src, dst, sem).start()

    def arrive(dst, sem):
        pltpu.make_async_copy(dst, dst, sem).wait()

    barrier = pltpu.get_barrier_semaphore()
    partners = [sibling]
    partners += [at(zz=lax.rem(z + i, NZ)) for i in range(1, NZ)]
    partners += [(dp, peer(i)) for i in range(1, NCTX)]
    partners += [(line, peer(i)) for i in range(NCTX)]
    for dev in partners:
        pl.semaphore_signal(barrier, inc=1, device_id=dev, device_id_type=MESH)
    local(wg_ref.at[0], packed.at[0:176], l_s.at[0])
    local(wg_ref.at[1], packed.at[176:352], l_s.at[0])
    local(wd_ref, packed.at[352:528], l_s.at[0])
    local(res_ref, res, l_s.at[1])
    arrive(packed, l_s.at[0])
    pl.semaphore_wait(barrier, len(partners))

    other_rows = pl.ds(pl.multiple_of((1 - core) * HALF_STEP, 16), HALF)
    send(packed.at[other_rows, :], oth, oth_s, oth_r, sibling)
    wo_part = wo_ref.at[:, cols(ctx * 256, 256)]
    for i in range(1, NZ):
        send(wo_part, wbuf.at[x, y, z, core], z_s, z_r, at(zz=lax.rem(z + i, NZ)))
    local(wo_part, wbuf.at[x, y, z, core], z_r)
    for i in range(1, NCTX):
        for j, ref in enumerate((q_ref, k_ref, v_ref)):
            send(ref.at[:, cols(peer(i) * HD, HD)], qkv.at[j, ctx], q_s, q_r.at[ctx], (dp, peer(i)))
    for j, ref in enumerate((q_ref, k_ref, v_ref)):
        local(ref.at[:, cols(ctx * HD, HD)], qkv.at[j, ctx], q_r.at[ctx])

    owners = (owner[0], owner[1])

    def weights():
        arrive(oth, oth_r)
        mate = dp + 1 - 2 * core
        own_rows = pl.ds(pl.multiple_of(core * HALF_STEP, 16), HALF)
        has = []
        for e in range(2):
            mine = owners[e] == dp
            mates = owners[e] == mate
            has.append(jnp.logical_or(mine, mates))
            for c in range(NZ):
                a = packed[own_rows, c * 128:(c + 1) * 128]
                b = oth[:, c * 128:(c + 1) * 128]
                cand[e, c] = lax.select(mine, a, lax.select(mates, b, jnp.zeros_like(b)))
        to = (up, down)
        for d in range(2):
            c = lax.rem(z + 8, NZ) if d == 0 else lax.rem(z + 9, NZ)
            for e in range(2):
                send(cand.at[e, c], rsb.at[e, HOPS * d], rs_s, rs_r.at[e, HOPS * d], to[d])
        yield
        for t in range(HOPS):
            for d in range(2):
                last = HOPS - 1 - d
                if t > last:
                    continue
                slot = HOPS * d + t
                c = lax.rem(z + 7 - t, NZ) if d == 0 else lax.rem(z + 10 + t, NZ)
                for e in range(2):
                    arrive(rsb.at[e, slot], rs_r.at[e, slot])
                    if t < last:
                        rsb[e, slot] = lax.select(has[e], cand[e, c], rsb[e, slot])
                        send(rsb.at[e, slot], rsb.at[e, slot + 1], rs_s, rs_r.at[e, slot + 1], to[d])
            yield

        def settled(e, known):
            met = rsb[e, HOPS - 1] + rsb[e, 2 * HOPS - 2]
            return lax.select(known, cand[e, z], met)

        known = jnp.where(xl == 0, has[1].astype(jnp.int32), has[0].astype(jnp.int32)) > 0
        xsend[...] = settled(1 - xl, known)
        send(xsend, xpiece, xp_s, xp_r, partner)
        known = jnp.where(xl == 0, has[0].astype(jnp.int32), has[1].astype(jnp.int32)) > 0
        here = settled(xl, known)
        arrive(xpiece, xp_r)
        wf[core, :, cols(z * 128, 128)] = here + xpiece[...]

        def piece(c):
            return wf.at[core, :, cols(c * 128, 128)]

        def part(c, h):
            return wf.at[core, pl.ds(AG_PARTS[h][0], AG_PARTS[h][1]), cols(c * 128, 128)]

        for h in range(2):
            for d in range(2):
                send(part(z, h), part(z, h), ag_s, ag_r.at[d, 0, h], to[d])
        send(piece(z), piece(z), cc_s, cc_r, sibling)
        yield
        for t in range(HOPS):
            for d in range(2):
                last = HOPS - 1 - d
                if t > last:
                    continue
                c = lax.rem(z + NZ - 1 - t, NZ) if d == 0 else lax.rem(z + 1 + t, NZ)
                for h in range(2):
                    arrive(part(c, h), ag_r.at[d, t, h])
                    if t < last:
                        send(part(c, h), part(c, h), ag_s, ag_r.at[d, t + 1, h], to[d])
                send(piece(c), piece(c), cc_s, cc_r, sibling)
            yield

    def a_slab(yy):
        return wbuf.at[:, yy, pl.ds(0, 8), core]

    def b_slab(xx):
        return wbuf.at[xx, :, pl.ds(8, 8), core]

    def main():
        arrive(wbuf.at[x, y, :, core], z_r)
        a_own = wbuf.at[x, y, pl.ds(0, 8), core]
        b_own = wbuf.at[x, y, pl.ds(8, 8), core]
        for i in range(1, 4):
            send(a_own, a_own, p1_s, p1_r.at[0], at(xx=lax.rem(x + i, NX)))
            send(b_own, b_own, p1_s, p1_r.at[1], at(yy=lax.rem(y + i, NY)))
        yield
        three = wbuf.at[pl.ds(0, 3), 0, pl.ds(0, 8), 0]
        arrive(three, p1_r.at[0])
        arrive(three, p1_r.at[1])
        for i in range(1, 4):
            send(a_slab(y), a_slab(y), p2_s, p2_r.at[0, y], at(yy=lax.rem(y + i, NY)))
            send(b_slab(x), b_slab(x), p2_s, p2_r.at[1, x], at(xx=lax.rem(x + i, NX)))
        send(a_slab(y), a_slab(y), c_s, c_r, sibling)
        send(b_slab(x), b_slab(x), c_s, c_r, sibling)
        yield
        for b in range(4):
            for i in (2 * b, 2 * b + 1):
                arrive(qkv.at[:, i], q_r.at[i])
            n = (b + 1) * 256
            q = qkv[0, 2 * b:2 * b + 2].reshape(256, HD)
            k = qkv[1, : 2 * b + 2].reshape(n, HD)
            v = qkv[2, : 2 * b + 2].reshape(n, HD)
            s = dot(q, k, NT) * HD ** (-0.5)
            qpos = lax.broadcasted_iota(jnp.int32, (256, n), 0) + b * 256
            kpos = lax.broadcasted_iota(jnp.int32, (256, n), 1)
            s = jnp.where(kpos <= qpos, s, -jnp.inf)
            w = jnp.exp(s - jnp.max(s, axis=1, keepdims=True))
            total = jnp.sum(w, axis=1, keepdims=True)
            o = dot(w.astype(BF), v) / total
            abuf[2 * b:2 * b + 2] = o.astype(BF).reshape(2, 128, HD)
            yield
        mine = attd.at[:, cols(ctx * HD, HD)]
        for i in range(1, NCTX):
            send(abuf.at[peer(i)], mine, a_s, a_r, (dp, peer(i)))
        local(abuf.at[ctx], mine, a_r)
        yield
        for i in (1, 3, 2):
            xx, yy = lax.rem(x + i, NX), lax.rem(y + i, NY)
            arrive(a_slab(yy), p2_r.at[0, yy])
            send(a_slab(yy), a_slab(yy), c_s, c_r, sibling)
            arrive(b_slab(xx), p2_r.at[1, xx])
            send(b_slab(xx), b_slab(xx), c_s, c_r, sibling)
            yield
        arrive(attd, a_r)
        arrive(res, l_s.at[1])
        arrive(wbuf.at[:, :, :, 1 - core], c_r)
        squares = jnp.zeros((TOK, 1), F32)
        for i in range(NCTX):
            acc = dot(attd[:, :512], wbuf[(i // NY) * 2, i % NY].reshape(512, 256))
            acc += dot(attd[:, 512:], wbuf[(i // NY) * 2 + 1, i % NY].reshape(512, 256))
            out = acc.astype(BF)
            here = slice(i * 256, (i + 1) * 256)
            proj_ref[:, here] = out
            combined = res[:, here].astype(F32) + out.astype(F32)
            squares += jnp.sum(combined * combined, axis=1, keepdims=True)
            if i % 4 == 3:
                yield
        scale = lax.rsqrt(squares * (1.0 / D) + EPSILON)
        for i in range(NCTX):
            here = slice(i * 256, (i + 1) * 256)
            combined = res[:, here].astype(F32) + proj_ref[:, here].astype(F32)
            normed[:, here] = (combined * scale * gain_ref[:, here]).astype(BF)
        for e, dst in ((xl, rbuf.at[xl, ctx]), (1 - xl, dsend)):
            first, second = slot_rows(ids_ref, jnp.where(e == 0, caps[0], caps[1]), e)
            rows = dot(first.astype(BF), normed[:, :1024]) + dot(second.astype(BF), normed[:, 1024:])
            dst[...] = rows.astype(BF)
        slot = rbuf.at[xl, ctx]
        for i in (4, 5, 6, 7, 1, 2, 3, 0):
            group = 0 if i >= 4 else 1
            if i:
                send(slot, slot, r_s.at[0], r_r.at[group], (dp, peer(i)))
            send(dsend, slot, r_s.at[1], r_r.at[group], (line, peer(i)))
        yield

    threads = {"w": weights(), "m": main()}
    for step in SCHEDULE:
        next(threads[step], 0)
    for step in ("m", "w"):
        for _ in threads[step]:
            pass

    arrive(wf.at[1 - core], cc_r)
    uw[0:80] = wf[0, 176:256]
    uw[80:176] = wf[1, 0:96]
    for g, group in enumerate(GROUPS):
        arrive(rbuf.at[0, pl.ds(0, 8 - g)], r_r.at[g])
        r = jnp.concatenate(
            [rbuf[s, peer(i)] for i in group for s in (xl, 1 - xl)], axis=0
        )
        pair = []
        for w in (wf.at[0, 0:176], uw):
            left = dot(r, w[:, :1024], NT).reshape(8, 48, FF_DEV)
            right = dot(r, w[:, 1024:], NT).reshape(8, 48, FF_DEV)
            pair.append((left[:, :CAP] + right[:, CAP:]).reshape(8 * CAP, FF_DEV))
        gate_proj, up_proj = pair
        hidden = (gate_proj / (1.0 + jnp.exp(-gate_proj)) * up_proj).astype(BF)
        halves = [
            dot(hidden, wf[1, 96:272, h * 1024:(h + 1) * 1024]).reshape(8, CAP, 1024)
            for h in range(2)
        ]
        out = jnp.concatenate(halves, axis=1).astype(BF)
        for j, i in enumerate(group):
            for s in range(2):
                sbuf[s, i] = out[2 * j + s]
        for i in group:
            if i:
                send(sbuf.at[0, i], pbuf.at[xl, ctx], e_s.at[0], e_r.at[0], (dp, peer(i)))
            send(sbuf.at[1, i], pbuf.at[xl, ctx], e_s.at[1], e_r.at[1], (line, peer(i)))

    arrive(pbuf.at[0, pl.ds(0, 7)], e_r.at[0])
    acc = sbuf[0, 0].astype(F32)
    for i in range(1, NCTX):
        acc += pbuf[xl, peer(i)].astype(F32)
    tot_ref[xl] = acc.astype(BF)
    arrive(pbuf.at[0], e_r.at[1])
    acc = pbuf[1 - xl, 0].astype(F32)
    for i in range(1, NCTX):
        acc += pbuf[1 - xl, i].astype(F32)
    tot_ref[1 - xl] = acc.astype(BF)

    arrive(oth, oth_s)
    arrive(wbuf.at[0, 0, pl.ds(0, NZ - 1), 0], z_s)
    arrive(qkv.at[:, pl.ds(0, NCTX - 1)], q_s)
    arrive(abuf.at[pl.ds(0, NCTX - 1)], a_s)
    arrive(wbuf.at[pl.ds(0, 3), pl.ds(0, 2), pl.ds(0, 8), 0], p1_s)
    arrive(wbuf.at[pl.ds(0, 3), :, :, 0], p2_s)
    arrive(wbuf.at[:, :, :, 0], c_s)
    arrive(rsb, rs_s)
    arrive(xsend, xp_s)
    arrive(wf.at[0, :, pl.ds(0, 15 * 128)], ag_s)
    arrive(wf.at[0], cc_s)
    for sems, buf in ((r_s, rbuf), (e_s, pbuf)):
        arrive(buf.at[0, pl.ds(0, 7)], sems.at[0])
        arrive(buf.at[0], sems.at[1])


def combine(caps, ids_ref, gates_ref, tot_ref, proj_ref, out_ref, sum_ref, sem):
    copy = pltpu.make_async_copy(proj_ref, out_ref, sem)
    copy.start()
    firsts, seconds, rows = [], [], []
    for e in range(2):
        gate = jnp.zeros((1, TOK), F32)
        for i in range(PICKS):
            gate += jnp.where(ids_ref[i] == e, gates_ref[i], 0.0)
        high = gate.astype(BF).astype(F32)
        first, second = slot_rows(ids_ref, caps[e], e)
        for g in (high, gate - high):
            firsts.append(first * g)
            seconds.append(second * g)
            rows.append(tot_ref[e])
    rows = jnp.concatenate(rows, axis=0)
    sum_ref[:, :1024] = dot(jnp.concatenate(firsts, axis=0).astype(BF), rows, TN).astype(BF)
    sum_ref[:, 1024:] = dot(jnp.concatenate(seconds, axis=0).astype(BF), rows, TN).astype(BF)
    copy.wait()


def body(
    query_vecs, key_vecs, value_vecs, residual, w_out, norm_gain, w_gate_up,
    w_down, expert_ids, route_gates, capacity, expert_owner,
):
    hbm = pl.BlockSpec(memory_space=pl.ANY)
    vmem = pl.BlockSpec(memory_space=pltpu.VMEM)
    smem = pl.BlockSpec(memory_space=pltpu.SMEM)
    dma = pltpu.SemaphoreType.DMA
    out = jax.ShapeDtypeStruct((TOK, D), BF)
    rows = (2 * CAP, 1024)
    ids = jnp.transpose(expert_ids, (2, 0, 1))
    gates = jnp.transpose(route_gates, (2, 0, 1))
    proj, tot = pl.pallas_call(
        kernel,
        out_shape=(out, jax.ShapeDtypeStruct((2,) + rows, BF)),
        in_specs=[smem, smem] + [hbm] * 7 + [vmem] * 2,
        out_specs=(vmem, vmem),
        scratch_shapes=[
            pltpu.VMEM((3, NCTX, TOK, HD), BF),
            pltpu.VMEM((NCTX, TOK, HD), BF),
            pltpu.VMEM((TOK, NCTX * HD), BF),
            pltpu.VMEM((NX, NY, NZ, 2, 16, 256), BF),
            pltpu.VMEM((TOK, D), BF),
            pltpu.VMEM((3 * FF_DEV, D), BF),
            pltpu.VMEM((HALF, D), BF),
            pltpu.VMEM((2, NZ, HALF, 128), BF),
            pltpu.VMEM((2, NZ - 1, HALF, 128), BF),
            pltpu.VMEM((HALF, 128), BF),
            pltpu.VMEM((HALF, 128), BF),
            pltpu.VMEM((2, HALF, D), BF),
            pltpu.VMEM((FF_DEV, D), BF),
            pltpu.VMEM((TOK, D), BF),
            pltpu.VMEM((2, NCTX) + rows, BF),
            pltpu.VMEM(rows, BF),
            pltpu.VMEM((2, NCTX) + rows, BF),
            pltpu.VMEM((2, NCTX) + rows, BF),
            dma, dma((NCTX,)), dma, dma, dma, dma,
            dma, dma((2,)), dma, dma((2, 4)), dma, dma,
            dma((2,)), dma, dma, dma, dma((2, NZ - 1)), dma, dma,
            dma, dma((2, HOPS, 2)), dma, dma,
            dma((2,)), dma((2,)), dma((2,)), dma((2,)),
        ],
        compiler_params=pltpu.CompilerParams(
            collective_id=0, has_side_effects=True, vmem_limit_bytes=58 << 20
        ),
    )(
        expert_owner[:2], capacity[0, 0],
        query_vecs[0], key_vecs[0], value_vecs[0], residual[0], w_out,
        jnp.swapaxes(w_gate_up[0], 1, 2), w_down[0], norm_gain[None], ids,
    )
    attn_proj, expert_sum = pl.pallas_call(
        combine,
        out_shape=(out, out),
        in_specs=[smem, vmem, vmem, vmem, hbm],
        out_specs=(hbm, vmem),
        scratch_shapes=[dma],
    )(capacity[0, 0], ids, gates, tot, proj)
    return (attn_proj[None], expert_sum[None])


def solution(mesh):
    seq = P("dp", "ctx", None)
    placed = (
        seq, seq, seq, seq, P("dp", None), P(),
        P("dp", None, None, "ctx"), seq, seq, seq, seq, P(),
    )
    return jax.shard_map(
        body, mesh=mesh, in_specs=placed, out_specs=(seq, seq), check_vma=False
    )
```

```python
import jax
import jax.numpy as jnp
from jax import lax
from jax.experimental import pallas as pl
from jax.experimental.pallas import tpu as pltpu
from jax.sharding import PartitionSpec as P

D = 2048
HD = 128
FF_DEV = 176
CAP = 24
TOK = 128
PICKS = 6
NZ = 16
NY = 4
NX = 4
NCTX = 8
HALF = 272
HALF_STEP = 256
HOPS = NZ // 2
EPSILON = 1e-06
MESH = pl.DeviceIdType.MESH
BF = jnp.bfloat16
F32 = jnp.float32

NN = (((1,), (0,)), ((), ()))
NT = (((1,), (1,)), ((), ()))
TN = (((0,), (0,)), ((), ()))

SCHEDULE = "wmwmwmwmmmmwmmmwmwmwmmmwwmwmwmwmwmwmwmwmw"
GROUPS = ((1, 2, 3, 4), (5, 6, 7, 0))
PARTS = ((0, 144), (144, 128))


def dot(a, b, dims=NN):
    return lax.dot_general(a, b, dims, preferred_element_type=F32)


def span(h):
    return pl.ds(*PARTS[h])


def cols(start, size):
    return pl.ds(pl.multiple_of(start, 128), size)


def slot_rows(ids_ref, cap, e):
    routed = jnp.zeros((1, TOK), F32)
    for i in range(PICKS):
        routed += jnp.where(ids_ref[i] == e, 1.0, 0.0)
    rows = lax.broadcasted_iota(jnp.int32, (TOK, TOK), 0)
    lanes = lax.broadcasted_iota(jnp.int32, (TOK, TOK), 1)
    before = jnp.where(rows < lanes, 1.0, 0.0).astype(BF)
    rank = dot(jnp.broadcast_to(routed, (8, TOK)).astype(BF), before)[0:1]
    kept = jnp.where(rank < cap.astype(F32), routed, 0.0)
    rank = jnp.where(kept > 0.5, rank, -1000.0)
    slot = lax.broadcasted_iota(jnp.int32, (2 * CAP, TOK), 0).astype(F32)
    first = jnp.where(rank == slot, 1.0, 0.0)
    second = jnp.where(rank == slot - CAP, 1.0, 0.0)
    return first, second


def kernel(
    owner, caps,
    q_ref, k_ref, v_ref, res_ref, wo_ref, wg_ref, wd_ref, gain_ref, ids_ref,
    proj_ref, tot_ref,
    qkv, abuf, attd, wbuf, res, packed, oth, cand, rsb, xsend, xpiece, wf, uw,
    normed, rbuf, dsend, sbuf, pbuf,
    q_s, q_r, a_s, a_r, z_s, z_r, p1_s, p1_r, p2_s, p2_r, c_s, c_r,
    l_s, oth_s, oth_r, rs_s, rs_r, xp_s, xp_r, ag_s, ag_r, cc_s, cc_r,
    r_s, r_r, e_s, e_r,
):
    dp = lax.axis_index("dp")
    ctx = lax.axis_index("ctx")
    core = lax.rem(dp, 2)
    z = lax.rem(dp // 2, NZ)
    xl = dp // (2 * NZ)
    xh = ctx // NY
    y = lax.rem(ctx, NY)
    x = xh * 2 + xl

    def at(xx=None, yy=None, zz=None, cc=None):
        xx = x if xx is None else xx
        yy = y if yy is None else yy
        zz = z if zz is None else zz
        cc = core if cc is None else cc
        return ((lax.rem(xx, 2) * NZ + zz) * 2 + cc, (xx // 2) * NY + yy)

    line = dp + 2 * NZ * (1 - 2 * xl)
    partner = (line, ctx)
    sibling = at(cc=1 - core)
    up = at(zz=lax.rem(z + 1, NZ))
    down = at(zz=lax.rem(z + NZ - 1, NZ))

    def peer(i):
        return lax.rem(ctx + i, NCTX)

    def send(src, dst, ssem, rsem, dev):
        pltpu.make_async_remote_copy(
            src_ref=src, dst_ref=dst, send_sem=ssem, recv_sem=rsem,
            device_id=dev, device_id_type=MESH,
        ).start()

    def local(src, dst, sem):
        pltpu.make_async_copy(src, dst, sem).start()

    def arrive(dst, sem):
        pltpu.make_async_copy(dst, dst, sem).wait()

    barrier = pltpu.get_barrier_semaphore()
    partners = [sibling]
    partners += [at(zz=lax.rem(z + i, NZ)) for i in range(1, NZ)]
    partners += [(dp, peer(i)) for i in range(1, NCTX)]
    partners += [(line, peer(i)) for i in range(NCTX)]
    for dev in partners:
        pl.semaphore_signal(barrier, inc=1, device_id=dev, device_id_type=MESH)
    local(wg_ref.at[0], packed.at[0:176], l_s.at[0])
    local(wg_ref.at[1], packed.at[176:352], l_s.at[0])
    local(wd_ref, packed.at[352:528], l_s.at[0])
    local(res_ref, res, l_s.at[1])
    arrive(packed, l_s.at[0])
    pl.semaphore_wait(barrier, len(partners))

    other_rows = pl.ds(pl.multiple_of((1 - core) * HALF_STEP, 16), HALF)
    send(packed.at[other_rows, :], oth, oth_s, oth_r, sibling)
    wo_part = wo_ref.at[:, cols(ctx * 256, 256)]
    for i in range(1, NZ):
        send(wo_part, wbuf.at[x, y, z, core], z_s, z_r, at(zz=lax.rem(z + i, NZ)))
    local(wo_part, wbuf.at[x, y, z, core], z_r)
    for i in range(1, NCTX):
        for j, ref in enumerate((q_ref, k_ref, v_ref)):
            send(ref.at[:, cols(peer(i) * HD, HD)], qkv.at[j, ctx], q_s, q_r.at[ctx], (dp, peer(i)))
    for j, ref in enumerate((q_ref, k_ref, v_ref)):
        local(ref.at[:, cols(ctx * HD, HD)], qkv.at[j, ctx], q_r.at[ctx])

    owners = (owner[0], owner[1])

    def weights():
        arrive(oth, oth_r)
        mate = dp + 1 - 2 * core
        own_rows = pl.ds(pl.multiple_of(core * HALF_STEP, 16), HALF)
        has = []
        for e in range(2):
            mine = owners[e] == dp
            mates = owners[e] == mate
            has.append(jnp.logical_or(mine, mates))
            for c in range(NZ):
                a = packed[own_rows, c * 128:(c + 1) * 128]
                b = oth[:, c * 128:(c + 1) * 128]
                cand[e, c] = lax.select(mine, a, lax.select(mates, b, jnp.zeros_like(b)))
        to = (up, down)
        for d in range(2):
            c = lax.rem(z + 8, NZ) if d == 0 else lax.rem(z + 9, NZ)
            for e in range(2):
                for h in range(2):
                    dst = rsb.at[e, HOPS * d, span(h)]
                    send(cand.at[e, c, span(h)], dst, rs_s, rs_r.at[e, HOPS * d, h], to[d])
        yield
        for t in range(HOPS):
            for d in range(2):
                last = HOPS - 1 - d
                if t > last:
                    continue
                slot = HOPS * d + t
                c = lax.rem(z + 7 - t, NZ) if d == 0 else lax.rem(z + 10 + t, NZ)
                for e in range(2):
                    for h in range(2):
                        got = rsb.at[e, slot, span(h)]
                        arrive(got, rs_r.at[e, slot, h])
                        if t < last:
                            got[...] = lax.select(has[e], cand[e, c, span(h)], got[...])
                            send(got, rsb.at[e, slot + 1, span(h)], rs_s, rs_r.at[e, slot + 1, h], to[d])
            yield

        def settled(e, known):
            met = rsb[e, HOPS - 1] + rsb[e, 2 * HOPS - 2]
            return lax.select(known, cand[e, z], met)

        known = jnp.where(xl == 0, has[1].astype(jnp.int32), has[0].astype(jnp.int32)) > 0
        xsend[...] = settled(1 - xl, known)
        send(xsend, xpiece, xp_s, xp_r, partner)
        known = jnp.where(xl == 0, has[0].astype(jnp.int32), has[1].astype(jnp.int32)) > 0
        here = settled(xl, known)
        arrive(xpiece, xp_r)
        wf[core, :, cols(z * 128, 128)] = here + xpiece[...]

        def piece(c):
            return wf.at[core, :, cols(c * 128, 128)]

        far = (at(zz=lax.rem(z + 2, NZ)), at(zz=lax.rem(z + NZ - 2, NZ)))

        def onward(c, d, t):
            if t < HOPS // 2 - d:
                send(piece(c), piece(c), ag_s.at[0], ag_r.at[d, 2 * t + 1], far[d])
            if t < HOPS // 2:
                send(piece(c), piece(c), ag_s.at[1], ag_r.at[d, 2 * t], to[d])
            send(piece(c), piece(c), cc_s, cc_r, sibling)

        def source(d, hops):
            return lax.rem(z + (NZ - hops if d == 0 else hops), NZ)

        for d in range(2):
            send(piece(z), piece(z), ag_s.at[0], ag_r.at[d, 1], far[d])
        for d in range(2):
            send(piece(z), piece(z), ag_s.at[1], ag_r.at[d, 0], to[d])
        send(piece(z), piece(z), cc_s, cc_r, sibling)
        yield
        for t in range(1, HOPS // 2 + 1):
            for d in range(2):
                if t <= HOPS // 2 - d:
                    c = source(d, 2 * t)
                    arrive(piece(c), ag_r.at[d, 2 * t - 1])
                    onward(c, d, t)
            yield
            for d in range(2):
                c = source(d, 2 * t - 1)
                arrive(piece(c), ag_r.at[d, 2 * t - 2])
                send(piece(c), piece(c), cc_s, cc_r, sibling)
            yield

    def a_slab(yy):
        return wbuf.at[:, yy, pl.ds(0, 8), core]

    def b_slab(xx):
        return wbuf.at[xx, :, pl.ds(8, 8), core]

    def main():
        arrive(wbuf.at[x, y, :, core], z_r)
        a_own = wbuf.at[x, y, pl.ds(0, 8), core]
        b_own = wbuf.at[x, y, pl.ds(8, 8), core]
        for i in range(1, 4):
            send(a_own, a_own, p1_s, p1_r.at[0], at(xx=lax.rem(x + i, NX)))
            send(b_own, b_own, p1_s, p1_r.at[1], at(yy=lax.rem(y + i, NY)))
        yield
        three = wbuf.at[pl.ds(0, 3), 0, pl.ds(0, 8), 0]
        arrive(three, p1_r.at[0])
        arrive(three, p1_r.at[1])
        for i in (1, 3, 2):
            send(a_slab(y), a_slab(y), p2_s, p2_r.at[0, y], at(yy=lax.rem(y + i, NY)))
            send(b_slab(x), b_slab(x), p2_s, p2_r.at[1, x], at(xx=lax.rem(x + i, NX)))
            yield
        send(a_slab(y), a_slab(y), c_s, c_r, sibling)
        send(b_slab(x), b_slab(x), c_s, c_r, sibling)
        yield
        for b in range(4):
            for i in (2 * b, 2 * b + 1):
                arrive(qkv.at[:, i], q_r.at[i])
            n = (b + 1) * 256
            q = qkv[0, 2 * b:2 * b + 2].reshape(256, HD)
            k = qkv[1, : 2 * b + 2].reshape(n, HD)
            v = qkv[2, : 2 * b + 2].reshape(n, HD)
            s = dot(q, k, NT) * HD ** (-0.5)
            qpos = lax.broadcasted_iota(jnp.int32, (256, n), 0) + b * 256
            kpos = lax.broadcasted_iota(jnp.int32, (256, n), 1)
            s = jnp.where(kpos <= qpos, s, -jnp.inf)
            w = jnp.exp(s - jnp.max(s, axis=1, keepdims=True))
            total = jnp.sum(w, axis=1, keepdims=True)
            o = dot(w.astype(BF), v) / total
            abuf[2 * b:2 * b + 2] = o.astype(BF).reshape(2, 128, HD)
            yield
        mine = attd.at[:, cols(ctx * HD, HD)]
        for i in range(1, NCTX):
            send(abuf.at[peer(i)], mine, a_s, a_r, (dp, peer(i)))
        local(abuf.at[ctx], mine, a_r)
        yield
        for i in (1, 3, 2):
            xx, yy = lax.rem(x + i, NX), lax.rem(y + i, NY)
            arrive(a_slab(yy), p2_r.at[0, yy])
            send(a_slab(yy), a_slab(yy), c_s, c_r, sibling)
            arrive(b_slab(xx), p2_r.at[1, xx])
            send(b_slab(xx), b_slab(xx), c_s, c_r, sibling)
            yield
        arrive(attd, a_r)
        arrive(res, l_s.at[1])
        arrive(wbuf.at[:, :, :, 1 - core], c_r)
        squares = jnp.zeros((TOK, 1), F32)
        for i in range(NCTX):
            acc = dot(attd[:, :512], wbuf[(i // NY) * 2, i % NY].reshape(512, 256))
            acc += dot(attd[:, 512:], wbuf[(i // NY) * 2 + 1, i % NY].reshape(512, 256))
            out = acc.astype(BF)
            here = slice(i * 256, (i + 1) * 256)
            proj_ref[:, here] = out
            combined = res[:, here].astype(F32) + out.astype(F32)
            squares += jnp.sum(combined * combined, axis=1, keepdims=True)
            if i % 4 == 3:
                yield
        scale = lax.rsqrt(squares * (1.0 / D) + EPSILON)
        for i in range(NCTX):
            here = slice(i * 256, (i + 1) * 256)
            combined = res[:, here].astype(F32) + proj_ref[:, here].astype(F32)
            normed[:, here] = (combined * scale * gain_ref[:, here]).astype(BF)
        for e, dst in ((xl, rbuf.at[xl, ctx]), (1 - xl, dsend)):
            first, second = slot_rows(ids_ref, jnp.where(e == 0, caps[0], caps[1]), e)
            rows = dot(first.astype(BF), normed[:, :1024]) + dot(second.astype(BF), normed[:, 1024:])
            dst[...] = rows.astype(BF)
        slot = rbuf.at[xl, ctx]
        for i in (4, 5, 6, 7, 1, 2, 3, 0):
            group = 0 if i >= 4 else 1
            if i:
                send(slot, slot, r_s.at[0], r_r.at[group], (dp, peer(i)))
            send(dsend, slot, r_s.at[1], r_r.at[group], (line, peer(i)))
            yield

    threads = {"w": weights(), "m": main()}
    for step in SCHEDULE:
        next(threads[step], 0)
    for step in ("m", "w"):
        for _ in threads[step]:
            pass

    arrive(wf.at[1 - core], cc_r)
    uw[0:80] = wf[0, 176:256]
    uw[80:176] = wf[1, 0:96]
    for g, group in enumerate(GROUPS):
        arrive(rbuf.at[0, pl.ds(0, 8 - g)], r_r.at[g])
        r = jnp.concatenate(
            [rbuf[s, peer(i)] for i in group for s in (xl, 1 - xl)], axis=0
        )
        pair = []
        for w in (wf.at[0, 0:176], uw):
            left = dot(r, w[:, :1024], NT).reshape(8, 48, FF_DEV)
            right = dot(r, w[:, 1024:], NT).reshape(8, 48, FF_DEV)
            pair.append((left[:, :CAP] + right[:, CAP:]).reshape(8 * CAP, FF_DEV))
        gate_proj, up_proj = pair
        hidden = (gate_proj / (1.0 + jnp.exp(-gate_proj)) * up_proj).astype(BF)
        halves = [
            dot(hidden, wf[1, 96:272, h * 1024:(h + 1) * 1024]).reshape(8, CAP, 1024)
            for h in range(2)
        ]
        out = jnp.concatenate(halves, axis=1).astype(BF)
        for j, i in enumerate(group):
            for s in range(2):
                sbuf[s, i] = out[2 * j + s]
        for i in group:
            if i:
                send(sbuf.at[0, i], pbuf.at[xl, ctx], e_s.at[0], e_r.at[0], (dp, peer(i)))
            send(sbuf.at[1, i], pbuf.at[xl, ctx], e_s.at[1], e_r.at[1], (line, peer(i)))

    arrive(pbuf.at[0, pl.ds(0, 7)], e_r.at[0])
    acc = sbuf[0, 0].astype(F32)
    for i in range(1, NCTX):
        acc += pbuf[xl, peer(i)].astype(F32)
    tot_ref[xl] = acc.astype(BF)
    arrive(pbuf.at[0], e_r.at[1])
    acc = pbuf[1 - xl, 0].astype(F32)
    for i in range(1, NCTX):
        acc += pbuf[1 - xl, i].astype(F32)
    tot_ref[1 - xl] = acc.astype(BF)

    arrive(oth, oth_s)
    arrive(wbuf.at[0, 0, pl.ds(0, NZ - 1), 0], z_s)
    arrive(qkv.at[:, pl.ds(0, NCTX - 1)], q_s)
    arrive(abuf.at[pl.ds(0, NCTX - 1)], a_s)
    arrive(wbuf.at[pl.ds(0, 3), pl.ds(0, 2), pl.ds(0, 8), 0], p1_s)
    arrive(wbuf.at[pl.ds(0, 3), :, :, 0], p2_s)
    arrive(wbuf.at[:, :, :, 0], c_s)
    arrive(rsb, rs_s)
    arrive(xsend, xp_s)
    arrive(wf.at[0, :, pl.ds(0, 7 * 128)], ag_s.at[0])
    arrive(wf.at[0, :, pl.ds(0, 8 * 128)], ag_s.at[1])
    arrive(wf.at[0], cc_s)
    for sems, buf in ((r_s, rbuf), (e_s, pbuf)):
        arrive(buf.at[0, pl.ds(0, 7)], sems.at[0])
        arrive(buf.at[0], sems.at[1])


def combine(caps, ids_ref, gates_ref, tot_ref, proj_ref, out_ref, sum_ref):
    out_ref[...] = proj_ref[...]
    firsts, seconds, rows = [], [], []
    for e in range(2):
        gate = jnp.zeros((1, TOK), F32)
        for i in range(PICKS):
            gate += jnp.where(ids_ref[i] == e, gates_ref[i], 0.0)
        high = gate.astype(BF).astype(F32)
        first, second = slot_rows(ids_ref, caps[e], e)
        for g in (high, gate - high):
            firsts.append(first * g)
            seconds.append(second * g)
            rows.append(tot_ref[e])
    rows = jnp.concatenate(rows, axis=0)
    sum_ref[:, :1024] = dot(jnp.concatenate(firsts, axis=0).astype(BF), rows, TN).astype(BF)
    sum_ref[:, 1024:] = dot(jnp.concatenate(seconds, axis=0).astype(BF), rows, TN).astype(BF)


def body(
    query_vecs, key_vecs, value_vecs, residual, w_out, norm_gain, w_gate_up,
    w_down, expert_ids, route_gates, capacity, expert_owner,
):
    hbm = pl.BlockSpec(memory_space=pl.ANY)
    vmem = pl.BlockSpec(memory_space=pltpu.VMEM)
    smem = pl.BlockSpec(memory_space=pltpu.SMEM)
    dma = pltpu.SemaphoreType.DMA
    out = jax.ShapeDtypeStruct((TOK, D), BF)
    rows = (2 * CAP, 1024)
    ids = jnp.transpose(expert_ids, (2, 0, 1))
    gates = jnp.transpose(route_gates, (2, 0, 1))
    proj, tot = pl.pallas_call(
        kernel,
        out_shape=(out, jax.ShapeDtypeStruct((2,) + rows, BF)),
        in_specs=[smem, smem] + [hbm] * 7 + [vmem] * 2,
        out_specs=(vmem, vmem),
        scratch_shapes=[
            pltpu.VMEM((3, NCTX, TOK, HD), BF),
            pltpu.VMEM((NCTX, TOK, HD), BF),
            pltpu.VMEM((TOK, NCTX * HD), BF),
            pltpu.VMEM((NX, NY, NZ, 2, 16, 256), BF),
            pltpu.VMEM((TOK, D), BF),
            pltpu.VMEM((3 * FF_DEV, D), BF),
            pltpu.VMEM((HALF, D), BF),
            pltpu.VMEM((2, NZ, HALF, 128), BF),
            pltpu.VMEM((2, NZ - 1, HALF, 128), BF),
            pltpu.VMEM((HALF, 128), BF),
            pltpu.VMEM((HALF, 128), BF),
            pltpu.VMEM((2, HALF, D), BF),
            pltpu.VMEM((FF_DEV, D), BF),
            pltpu.VMEM((TOK, D), BF),
            pltpu.VMEM((2, NCTX) + rows, BF),
            pltpu.VMEM(rows, BF),
            pltpu.VMEM((2, NCTX) + rows, BF),
            pltpu.VMEM((2, NCTX) + rows, BF),
            dma, dma((NCTX,)), dma, dma, dma, dma,
            dma, dma((2,)), dma, dma((2, 4)), dma, dma,
            dma((2,)), dma, dma, dma, dma((2, NZ - 1, 2)), dma, dma,
            dma((2,)), dma((2, HOPS)), dma, dma,
            dma((2,)), dma((2,)), dma((2,)), dma((2,)),
        ],
        compiler_params=pltpu.CompilerParams(
            collective_id=0, has_side_effects=True, vmem_limit_bytes=58 << 20
        ),
    )(
        expert_owner[:2], capacity[0, 0],
        query_vecs[0], key_vecs[0], value_vecs[0], residual[0], w_out,
        jnp.swapaxes(w_gate_up[0], 1, 2), w_down[0], norm_gain[None], ids,
    )
    attn_proj, expert_sum = pl.pallas_call(
        combine,
        out_shape=(out, out),
        in_specs=[smem] + [vmem] * 4,
        out_specs=(vmem, vmem),
    )(capacity[0, 0], ids, gates, tot, proj)
    return (attn_proj[None], expert_sum[None])


def solution(mesh):
    seq = P("dp", "ctx", None)
    placed = (
        seq, seq, seq, seq, P("dp", None), P(),
        P("dp", None, None, "ctx"), seq, seq, seq, seq, P(),
    )
    return jax.shard_map(
        body, mesh=mesh, in_specs=placed, out_specs=(seq, seq), check_vma=False
    )
```

```python
import jax
import jax.numpy as jnp
from jax import lax
from jax.experimental import pallas as pl
from jax.experimental.pallas import tpu as pltpu
from jax.sharding import PartitionSpec as P

D = 2048
HD = 128
FF_DEV = 176
CAP = 24
TOK = 128
PICKS = 6
NZ = 16
NY = 4
NX = 4
NCTX = 8
HALF = 272
HALF_STEP = 256
HOPS = NZ // 2
EPSILON = 1e-06
MESH = pl.DeviceIdType.MESH
BF = jnp.bfloat16
F32 = jnp.float32

NN = (((1,), (0,)), ((), ()))
NT = (((1,), (1,)), ((), ()))
TN = (((0,), (0,)), ((), ()))

SCHEDULE = "mwmwmwmwmwmmmmwmmmwmwmwwmmmwmwmwmwmwmwmwmwm"
GROUPS = ((1, 2, 5, 6), (3, 0, 7, 4))
PARTS = ((0, 144), (144, 128))


def dot(a, b, dims=NN):
    return lax.dot_general(a, b, dims, preferred_element_type=F32)


def span(h):
    return pl.ds(*PARTS[h])


def cols(start, size):
    return pl.ds(pl.multiple_of(start, 128), size)


def slot_rows(ids_ref, cap, e):
    routed = jnp.zeros((1, TOK), F32)
    for i in range(PICKS):
        routed += jnp.where(ids_ref[i] == e, 1.0, 0.0)
    rows = lax.broadcasted_iota(jnp.int32, (TOK, TOK), 0)
    lanes = lax.broadcasted_iota(jnp.int32, (TOK, TOK), 1)
    before = jnp.where(rows < lanes, 1.0, 0.0).astype(BF)
    rank = dot(jnp.broadcast_to(routed, (8, TOK)).astype(BF), before)[0:1]
    kept = jnp.where(rank < cap.astype(F32), routed, 0.0)
    rank = jnp.where(kept > 0.5, rank, -1000.0)
    slot = lax.broadcasted_iota(jnp.int32, (2 * CAP, TOK), 0).astype(F32)
    first = jnp.where(rank == slot, 1.0, 0.0)
    second = jnp.where(rank == slot - CAP, 1.0, 0.0)
    return first, second


def kernel(
    owner, caps,
    q_ref, k_ref, v_ref, res_ref, wo_ref, wg_ref, wd_ref, gain_ref, ids_ref,
    proj_ref, tot_ref,
    qkv, abuf, attd, wbuf, res, packed, early, lead, oth, cand, rsb, xsend, xpiece, wf, uw,
    normed, rbuf, dsend, sbuf, a1, b1, sa, sb, a2, b2,
    q_s, q_r, a_s, a_r, z_s, z_r, p1_s, p1_r, p2_s, p2_r, c_s, c_r,
    l_s, early_s, early_r, oth_s, oth_r, rs_s, rs_r, xp_s, xp_r, ag_s, ag_r, cc_s, cc_r,
    r_s, r_r, e_s, e_r,
):
    dp = lax.axis_index("dp")
    ctx = lax.axis_index("ctx")
    core = lax.rem(dp, 2)
    z = lax.rem(dp // 2, NZ)
    xl = dp // (2 * NZ)
    xh = ctx // NY
    y = lax.rem(ctx, NY)
    x = xh * 2 + xl

    def at(xx=None, yy=None, zz=None, cc=None):
        xx = x if xx is None else xx
        yy = y if yy is None else yy
        zz = z if zz is None else zz
        cc = core if cc is None else cc
        return ((lax.rem(xx, 2) * NZ + zz) * 2 + cc, (xx // 2) * NY + yy)

    line = dp + 2 * NZ * (1 - 2 * xl)
    partner = (line, ctx)
    sibling = at(cc=1 - core)
    up = at(zz=lax.rem(z + 1, NZ))
    down = at(zz=lax.rem(z + NZ - 1, NZ))

    def peer(i):
        return lax.rem(xh + i // NY, 2) * NY + lax.rem(y + i % NY, NY)

    def send(src, dst, ssem, rsem, dev):
        pltpu.make_async_remote_copy(
            src_ref=src, dst_ref=dst, send_sem=ssem, recv_sem=rsem,
            device_id=dev, device_id_type=MESH,
        ).start()

    def local(src, dst, sem):
        pltpu.make_async_copy(src, dst, sem).start()

    def arrive(dst, sem):
        pltpu.make_async_copy(dst, dst, sem).wait()

    barrier = pltpu.get_barrier_semaphore()
    near = (1, 15, 2, 14, 3, 13, 4, 12)
    partners = [sibling]
    partners += [at(zz=lax.rem(z + i, NZ)) for i in near]
    partners += [(dp, peer(i)) for i in range(1, NCTX)]
    partners += [(line, peer(i)) for i in range(NCTX)]
    for dev in partners:
        pl.semaphore_signal(barrier, inc=1, device_id=dev, device_id_type=MESH)
    local(wg_ref.at[0], packed.at[0:176], l_s.at[0])
    local(wg_ref.at[1], packed.at[176:352], l_s.at[0])
    local(wd_ref, packed.at[352:528], l_s.at[0])
    local(res_ref, res, l_s.at[1])
    arrive(packed, l_s.at[0])
    pl.semaphore_wait(barrier, len(partners))

    other_rows = pl.ds(pl.multiple_of((1 - core) * HALF_STEP, 16), HALF)
    firsts = (lax.rem(z + 8, NZ), lax.rem(z + 9, NZ))
    for d in range(2):
        send(packed.at[other_rows, cols(firsts[d] * 128, 128)], early.at[d], early_s, early_r, sibling)
    send(packed.at[other_rows, :], oth, oth_s, oth_r, sibling)
    wo_part = wo_ref.at[:, cols(ctx * 256, 256)]
    for i in near:
        send(wo_part, wbuf.at[x, y, z, core], z_s.at[0], z_r.at[0], at(zz=lax.rem(z + i, NZ)))
    local(wo_part, wbuf.at[x, y, z, core], z_r.at[0])
    owners = (owner[0], owner[1])

    def weights():
        mate = dp + 1 - 2 * core
        own_rows = pl.ds(pl.multiple_of(core * HALF_STEP, 16), HALF)
        mine = [owners[e] == dp for e in range(2)]
        mates = [owners[e] == mate for e in range(2)]
        has = [jnp.logical_or(mine[e], mates[e]) for e in range(2)]

        def pick(e, a, b):
            return lax.select(mine[e], a, lax.select(mates[e], b, jnp.zeros_like(b)))

        to = (up, down)
        arrive(early, early_r)
        for d in range(2):
            a = packed[own_rows, cols(firsts[d] * 128, 128)]
            for e in range(2):
                lead[e, d] = pick(e, a, early[d])
                for h in range(2):
                    dst = rsb.at[e, HOPS * d, span(h)]
                    send(lead.at[e, d, span(h)], dst, rs_s, rs_r.at[e, HOPS * d, h], to[d])
        yield
        arrive(oth, oth_r)
        for c in range(NZ):
            a = packed[own_rows, c * 128:(c + 1) * 128]
            b = oth[:, c * 128:(c + 1) * 128]
            for e in range(2):
                cand[e, c] = pick(e, a, b)
        for t in range(HOPS):
            for d in range(2):
                last = HOPS - 1 - d
                if t > last:
                    continue
                slot = HOPS * d + t
                c = lax.rem(z + 7 - t, NZ) if d == 0 else lax.rem(z + 10 + t, NZ)
                for e in range(2):
                    for h in range(2):
                        got = rsb.at[e, slot, span(h)]
                        arrive(got, rs_r.at[e, slot, h])
                        if t < last:
                            got[...] = lax.select(has[e], cand[e, c, span(h)], got[...])
                            send(got, rsb.at[e, slot + 1, span(h)], rs_s, rs_r.at[e, slot + 1, h], to[d])
            yield

        def settled(e, known):
            met = rsb[e, HOPS - 1] + rsb[e, 2 * HOPS - 2]
            return lax.select(known, cand[e, z], met)

        known = jnp.where(xl == 0, has[1].astype(jnp.int32), has[0].astype(jnp.int32)) > 0
        xsend[...] = settled(1 - xl, known)
        send(xsend, xpiece, xp_s, xp_r, partner)
        known = jnp.where(xl == 0, has[0].astype(jnp.int32), has[1].astype(jnp.int32)) > 0
        here = settled(xl, known)
        arrive(xpiece, xp_r)
        wf[core, :, cols(z * 128, 128)] = here + xpiece[...]

        def piece(c):
            return wf.at[core, :, cols(c * 128, 128)]

        far = (at(zz=lax.rem(z + 2, NZ)), at(zz=lax.rem(z + NZ - 2, NZ)))

        def onward(c, d, t):
            if t < HOPS // 2 - d:
                send(piece(c), piece(c), ag_s.at[0], ag_r.at[d, 2 * t + 1], far[d])
            if t < HOPS // 2:
                send(piece(c), piece(c), ag_s.at[1], ag_r.at[d, 2 * t], to[d])
            send(piece(c), piece(c), cc_s, cc_r, sibling)

        def source(d, hops):
            return lax.rem(z + (NZ - hops if d == 0 else hops), NZ)

        for d in range(2):
            send(piece(z), piece(z), ag_s.at[0], ag_r.at[d, 1], far[d])
        for d in range(2):
            send(piece(z), piece(z), ag_s.at[1], ag_r.at[d, 0], to[d])
        send(piece(z), piece(z), cc_s, cc_r, sibling)
        yield
        for t in range(1, HOPS // 2 + 1):
            for d in range(2):
                if t <= HOPS // 2 - d:
                    c = source(d, 2 * t)
                    arrive(piece(c), ag_r.at[d, 2 * t - 1])
                    onward(c, d, t)
            yield
            for d in range(2):
                c = source(d, 2 * t - 1)
                arrive(piece(c), ag_r.at[d, 2 * t - 2])
                send(piece(c), piece(c), cc_s, cc_r, sibling)
            yield

    def a_slab(yy):
        return wbuf.at[:, yy, pl.ds(0, 8), core]

    def b_slab(xx):
        return wbuf.at[xx, :, pl.ds(8, 8), core]

    def main():
        for i in range(1, NCTX):
            for j, ref in enumerate((q_ref, k_ref, v_ref)):
                send(ref.at[:, cols(peer(i) * HD, HD)], qkv.at[j, ctx], q_s, q_r.at[ctx], (dp, peer(i)))
        for j, ref in enumerate((q_ref, k_ref, v_ref)):
            local(ref.at[:, cols(ctx * HD, HD)], qkv.at[j, ctx], q_r.at[ctx])
        yield
        arrive(wbuf.at[0, 0, pl.ds(0, 9), 0], z_r.at[0])
        for i in (1, 2, 3, 4):
            block = wbuf.at[x, y, lax.rem(z + NZ - i, NZ), core]
            send(block, block, z_s.at[1], z_r.at[1], at(zz=lax.rem(z + 4, NZ)))
            if i < 4:
                block = wbuf.at[x, y, lax.rem(z + i, NZ), core]
                send(block, block, z_s.at[1], z_r.at[1], at(zz=lax.rem(z + 12, NZ)))
        yield
        arrive(wbuf.at[0, 0, pl.ds(0, 7), 0], z_r.at[1])
        a_own = wbuf.at[x, y, pl.ds(0, 8), core]
        b_own = wbuf.at[x, y, pl.ds(8, 8), core]
        for i in range(1, 4):
            send(a_own, a_own, p1_s, p1_r.at[0], at(xx=lax.rem(x + i, NX)))
            send(b_own, b_own, p1_s, p1_r.at[1], at(yy=lax.rem(y + i, NY)))
        yield
        three = wbuf.at[pl.ds(0, 3), 0, pl.ds(0, 8), 0]
        arrive(three, p1_r.at[0])
        arrive(three, p1_r.at[1])
        for i in (1, 3, 2):
            send(a_slab(y), a_slab(y), p2_s, p2_r.at[0, y], at(yy=lax.rem(y + i, NY)))
            send(b_slab(x), b_slab(x), p2_s, p2_r.at[1, x], at(xx=lax.rem(x + i, NX)))
            yield
        send(a_slab(y), a_slab(y), c_s, c_r, sibling)
        send(b_slab(x), b_slab(x), c_s, c_r, sibling)
        yield
        for b in range(4):
            for i in (2 * b, 2 * b + 1):
                arrive(qkv.at[:, i], q_r.at[i])
            n = (b + 1) * 256
            q = qkv[0, 2 * b:2 * b + 2].reshape(256, HD)
            k = qkv[1, : 2 * b + 2].reshape(n, HD)
            v = qkv[2, : 2 * b + 2].reshape(n, HD)
            s = dot(q, k, NT) * HD ** (-0.5)
            qpos = lax.broadcasted_iota(jnp.int32, (256, n), 0) + b * 256
            kpos = lax.broadcasted_iota(jnp.int32, (256, n), 1)
            s = jnp.where(kpos <= qpos, s, -jnp.inf)
            w = jnp.exp(s - jnp.max(s, axis=1, keepdims=True))
            total = jnp.sum(w, axis=1, keepdims=True)
            o = dot(w.astype(BF), v) / total
            abuf[2 * b:2 * b + 2] = o.astype(BF).reshape(2, 128, HD)
            yield
        mine = attd.at[:, cols(ctx * HD, HD)]
        for i in range(1, NCTX):
            send(abuf.at[peer(i)], mine, a_s, a_r, (dp, peer(i)))
        local(abuf.at[ctx], mine, a_r)
        yield
        for i in (1, 3, 2):
            xx, yy = lax.rem(x + i, NX), lax.rem(y + i, NY)
            arrive(a_slab(yy), p2_r.at[0, yy])
            send(a_slab(yy), a_slab(yy), c_s, c_r, sibling)
            arrive(b_slab(xx), p2_r.at[1, xx])
            send(b_slab(xx), b_slab(xx), c_s, c_r, sibling)
            yield
        arrive(attd, a_r)
        arrive(res, l_s.at[1])
        arrive(wbuf.at[:, :, :, 1 - core], c_r)
        squares = jnp.zeros((TOK, 1), F32)
        for i in range(NCTX):
            acc = dot(attd[:, :512], wbuf[(i // NY) * 2, i % NY].reshape(512, 256))
            acc += dot(attd[:, 512:], wbuf[(i // NY) * 2 + 1, i % NY].reshape(512, 256))
            out = acc.astype(BF)
            here = slice(i * 256, (i + 1) * 256)
            proj_ref[:, here] = out
            combined = res[:, here].astype(F32) + out.astype(F32)
            squares += jnp.sum(combined * combined, axis=1, keepdims=True)
            if i % 4 == 3:
                yield
        scale = lax.rsqrt(squares * (1.0 / D) + EPSILON)
        for i in range(NCTX):
            here = slice(i * 256, (i + 1) * 256)
            combined = res[:, here].astype(F32) + proj_ref[:, here].astype(F32)
            normed[:, here] = (combined * scale * gain_ref[:, here]).astype(BF)
        for e, dst in ((xl, rbuf.at[xl, ctx]), (1 - xl, dsend)):
            first, second = slot_rows(ids_ref, jnp.where(e == 0, caps[0], caps[1]), e)
            rows = dot(first.astype(BF), normed[:, :1024]) + dot(second.astype(BF), normed[:, 1024:])
            dst[...] = rows.astype(BF)
        slot = rbuf.at[xl, ctx]
        for i in (2, 6, 3, 7, 1, 5, 4, 0):
            group = 0 if i % NY >= 2 else 1
            if i:
                send(slot, slot, r_s.at[0], r_r.at[group], (dp, peer(i)))
            send(dsend, slot, r_s.at[1], r_r.at[group], (line, peer(i)))
            yield

    threads = {"w": weights(), "m": main()}
    for step in SCHEDULE:
        next(threads[step], 0)
    for step in ("m", "w"):
        for _ in threads[step]:
            pass

    arrive(wf.at[1 - core], cc_r)
    uw[0:80] = wf[0, 176:256]
    uw[80:176] = wf[1, 0:96]
    for g, group in enumerate(GROUPS):
        arrive(rbuf.at[0, pl.ds(0, 8 - g)], r_r.at[g])
        r = jnp.concatenate(
            [rbuf[s, peer(i)] for i in group for s in (xl, 1 - xl)], axis=0
        )
        pair = []
        for w in (wf.at[0, 0:176], uw):
            left = dot(r, w[:, :1024], NT).reshape(8, 48, FF_DEV)
            right = dot(r, w[:, 1024:], NT).reshape(8, 48, FF_DEV)
            pair.append((left[:, :CAP] + right[:, CAP:]).reshape(8 * CAP, FF_DEV))
        gate_proj, up_proj = pair
        hidden = (gate_proj / (1.0 + jnp.exp(-gate_proj)) * up_proj).astype(BF)
        halves = [
            dot(hidden, wf[1, 96:272, h * 1024:(h + 1) * 1024]).reshape(8, CAP, 1024)
            for h in range(2)
        ]
        out = jnp.concatenate(halves, axis=1).astype(BF)
        for j, i in enumerate(group):
            for s in range(2):
                xx = lax.rem(xh + i // NY, 2) * 2 + (xl if s == 0 else 1 - xl)
                for h in range(2):
                    sbuf[h, xx, lax.rem(y + i % NY, NY)] = out[2 * j + s, :, h * 512:(h + 1) * 512]
        for i in ((1, 2), (3,))[g]:
            yy = lax.rem(y + i, NY)
            send(sbuf.at[0, :, yy], a1.at[y], e_s.at[0], e_r.at[0], at(yy=yy))

    across = [lax.rem(x + i, NX) for i in range(NX)]
    along = [lax.rem(y + i, NY) for i in range(NY)]
    for i in (1, 3, 2):
        send(sbuf.at[1, across[i]], b1.at[x], e_s.at[1], e_r.at[1], at(xx=across[i]))

    def wide(*parts):
        acc = parts[0].astype(F32)
        for part in parts[1:]:
            acc += part.astype(F32)
        return acc.astype(BF)

    arrive(a1.at[pl.ds(0, 3)], e_r.at[0])
    for i in (2, 1, 3, 0):
        xx = across[i]
        sa[xx] = wide(sbuf[0, xx, y], *[a1[along[j], xx] for j in range(1, NY)])
        if i:
            send(sa.at[xx], a2.at[x], e_s.at[2], e_r.at[2], at(xx=xx))
    arrive(b1.at[pl.ds(0, 3)], e_r.at[1])
    for i in (2, 1, 3, 0):
        yy = along[i]
        sb[yy, 0] = wide(sbuf[1, x, yy], b1[across[2], yy])
        sb[yy, 1] = wide(b1[across[1], yy], b1[across[3], yy])
        if i:
            send(sb.at[yy], b2.at[y], e_s.at[3], e_r.at[3], at(yy=yy))
    arrive(a2.at[pl.ds(0, 3)], e_r.at[2])
    tot_ref[xl, :, :512] = wide(sa[x], a2[across[2]])
    tot_ref[1 - xl, :, :512] = wide(a2[across[1]], a2[across[3]])
    arrive(b2.at[pl.ds(0, 3)], e_r.at[3])
    for s, e in ((0, xl), (1, 1 - xl)):
        tot_ref[e, :, 512:] = wide(sb[y, s], *[b2[along[j], s] for j in range(1, NY)])

    arrive(early, early_s)
    arrive(oth, oth_s)
    arrive(wbuf.at[0, 0, pl.ds(0, 8), 0], z_s.at[0])
    arrive(wbuf.at[0, 0, pl.ds(0, 7), 0], z_s.at[1])
    arrive(qkv.at[:, pl.ds(0, NCTX - 1)], q_s)
    arrive(abuf.at[pl.ds(0, NCTX - 1)], a_s)
    arrive(wbuf.at[pl.ds(0, 3), pl.ds(0, 2), pl.ds(0, 8), 0], p1_s)
    arrive(wbuf.at[pl.ds(0, 3), :, :, 0], p2_s)
    arrive(wbuf.at[:, :, :, 0], c_s)
    arrive(rsb, rs_s)
    arrive(xsend, xp_s)
    arrive(wf.at[0, :, pl.ds(0, 7 * 128)], ag_s.at[0])
    arrive(wf.at[0, :, pl.ds(0, 8 * 128)], ag_s.at[1])
    arrive(wf.at[0], cc_s)
    arrive(rbuf.at[0, pl.ds(0, 7)], r_s.at[0])
    arrive(rbuf.at[0], r_s.at[1])
    for i, buf in enumerate((a1, b1, a2, b2)):
        arrive(buf.at[pl.ds(0, 3)], e_s.at[i])


def combine(caps, ids_ref, gates_ref, tot_ref, proj_ref, out_ref, sum_ref):
    out_ref[...] = proj_ref[...]
    firsts, seconds, rows = [], [], []
    for e in range(2):
        gate = jnp.zeros((1, TOK), F32)
        for i in range(PICKS):
            gate += jnp.where(ids_ref[i] == e, gates_ref[i], 0.0)
        high = gate.astype(BF).astype(F32)
        first, second = slot_rows(ids_ref, caps[e], e)
        for g in (high, gate - high):
            firsts.append(first * g)
            seconds.append(second * g)
            rows.append(tot_ref[e])
    rows = jnp.concatenate(rows, axis=0)
    sum_ref[:, :1024] = dot(jnp.concatenate(firsts, axis=0).astype(BF), rows, TN).astype(BF)
    sum_ref[:, 1024:] = dot(jnp.concatenate(seconds, axis=0).astype(BF), rows, TN).astype(BF)


def body(
    query_vecs, key_vecs, value_vecs, residual, w_out, norm_gain, w_gate_up,
    w_down, expert_ids, route_gates, capacity, expert_owner,
):
    hbm = pl.BlockSpec(memory_space=pl.ANY)
    vmem = pl.BlockSpec(memory_space=pltpu.VMEM)
    smem = pl.BlockSpec(memory_space=pltpu.SMEM)
    dma = pltpu.SemaphoreType.DMA
    out = jax.ShapeDtypeStruct((TOK, D), BF)
    rows = (2 * CAP, 1024)
    half = (2 * CAP, 512)
    ids = jnp.transpose(expert_ids, (2, 0, 1))
    gates = jnp.transpose(route_gates, (2, 0, 1))
    proj, tot = pl.pallas_call(
        kernel,
        out_shape=(out, jax.ShapeDtypeStruct((2,) + rows, BF)),
        in_specs=[smem, smem] + [hbm] * 7 + [vmem] * 2,
        out_specs=(vmem, vmem),
        scratch_shapes=[
            pltpu.VMEM((3, NCTX, TOK, HD), BF),
            pltpu.VMEM((NCTX, TOK, HD), BF),
            pltpu.VMEM((TOK, NCTX * HD), BF),
            pltpu.VMEM((NX, NY, NZ, 2, 16, 256), BF),
            pltpu.VMEM((TOK, D), BF),
            pltpu.VMEM((3 * FF_DEV, D), BF),
            pltpu.VMEM((2, HALF, 128), BF),
            pltpu.VMEM((2, 2, HALF, 128), BF),
            pltpu.VMEM((HALF, D), BF),
            pltpu.VMEM((2, NZ, HALF, 128), BF),
            pltpu.VMEM((2, NZ - 1, HALF, 128), BF),
            pltpu.VMEM((HALF, 128), BF),
            pltpu.VMEM((HALF, 128), BF),
            pltpu.VMEM((2, HALF, D), BF),
            pltpu.VMEM((FF_DEV, D), BF),
            pltpu.VMEM((TOK, D), BF),
            pltpu.VMEM((2, NCTX) + rows, BF),
            pltpu.VMEM(rows, BF),
            pltpu.VMEM((2, NX, NY) + half, BF),
            pltpu.VMEM((NY, NX) + half, BF),
            pltpu.VMEM((NX, NY) + half, BF),
            pltpu.VMEM((NX,) + half, BF),
            pltpu.VMEM((NY, 2) + half, BF),
            pltpu.VMEM((NX,) + half, BF),
            pltpu.VMEM((NY, 2) + half, BF),
            dma, dma((NCTX,)), dma, dma, dma((2,)), dma((2,)),
            dma, dma((2,)), dma, dma((2, 4)), dma, dma,
            dma((2,)), dma, dma, dma, dma, dma, dma((2, NZ - 1, 2)), dma, dma,
            dma((2,)), dma((2, HOPS)), dma, dma,
            dma((2,)), dma((2,)), dma((4,)), dma((4,)),
        ],
        compiler_params=pltpu.CompilerParams(
            collective_id=0, has_side_effects=True, vmem_limit_bytes=58 << 20
        ),
    )(
        expert_owner[:2], capacity[0, 0],
        query_vecs[0], key_vecs[0], value_vecs[0], residual[0], w_out,
        jnp.swapaxes(w_gate_up[0], 1, 2), w_down[0], norm_gain[None], ids,
    )
    attn_proj, expert_sum = pl.pallas_call(
        combine,
        out_shape=(out, out),
        in_specs=[smem] + [vmem] * 4,
        out_specs=(vmem, vmem),
    )(capacity[0, 0], ids, gates, tot, proj)
    return (attn_proj[None], expert_sum[None])


def solution(mesh):
    seq = P("dp", "ctx", None)
    placed = (
        seq, seq, seq, seq, P("dp", None), P(),
        P("dp", None, None, "ctx"), seq, seq, seq, seq, P(),
    )
    return jax.shard_map(
        body, mesh=mesh, in_specs=placed, out_specs=(seq, seq), check_vma=False
    )
```

```python
import jax
import jax.numpy as jnp
from jax import lax
from jax.experimental import pallas as pl
from jax.experimental.pallas import tpu as pltpu
from jax.sharding import PartitionSpec as P

D = 2048
HD = 128
FF_DEV = 176
CAP = 24
TOK = 128
PICKS = 6
NZ = 16
NY = 4
NX = 4
NCTX = 8
HALF = 272
HALF_STEP = 256
HOPS = NZ // 2
EPSILON = 1e-06
MESH = pl.DeviceIdType.MESH
BF = jnp.bfloat16
F32 = jnp.float32

NN = (((1,), (0,)), ((), ()))
NT = (((1,), (1,)), ((), ()))
TN = (((0,), (0,)), ((), ()))

SCHEDULE = "mwmwmwmwmwmmmmwmmmwmwmwmwmmmwmwmwmwmwmwmwmw"
GROUPS = ((1, 2, 5, 6), (3, 0, 7, 4))
PARTS = ((0, 144), (144, 128))


def dot(a, b, dims=NN):
    return lax.dot_general(a, b, dims, preferred_element_type=F32)


def span(h):
    return pl.ds(*PARTS[h])


def cols(start, size):
    return pl.ds(pl.multiple_of(start, 128), size)


def slot_rows(ids_ref, cap, e):
    routed = jnp.zeros((1, TOK), F32)
    for i in range(PICKS):
        routed += jnp.where(ids_ref[i] == e, 1.0, 0.0)
    rows = lax.broadcasted_iota(jnp.int32, (TOK, TOK), 0)
    lanes = lax.broadcasted_iota(jnp.int32, (TOK, TOK), 1)
    before = jnp.where(rows < lanes, 1.0, 0.0).astype(BF)
    rank = dot(jnp.broadcast_to(routed, (8, TOK)).astype(BF), before)[0:1]
    kept = jnp.where(rank < cap.astype(F32), routed, 0.0)
    rank = jnp.where(kept > 0.5, rank, -1000.0)
    slot = lax.broadcasted_iota(jnp.int32, (2 * CAP, TOK), 0).astype(F32)
    first = jnp.where(rank == slot, 1.0, 0.0)
    second = jnp.where(rank == slot - CAP, 1.0, 0.0)
    return first, second


def kernel(
    owner, caps,
    q_ref, k_ref, v_ref, res_ref, wo_ref, wg_ref, wd_ref, gain_ref, ids_ref,
    proj_ref, tot_ref,
    qkv, abuf, attd, wbuf, res, packed, early, lead, oth, cand, rsb, xsend, xpiece, wf, uw,
    normed, rbuf, dsend, sbuf, a1, b1, sa, sb, a2, b2,
    q_s, q_r, a_s, a_r, z_s, z_r, p1_s, p1_r, p2_s, p2_r, c_s, c_r,
    l_s, early_s, early_r, oth_s, oth_r, rs_s, rs_r, xp_s, xp_r, ag_s, ag_r, cc_s, cc_r,
    r_s, r_r, e_s, e_r,
):
    dp = lax.axis_index("dp")
    ctx = lax.axis_index("ctx")
    core = lax.rem(dp, 2)
    z = lax.rem(dp // 2, NZ)
    xl = dp // (2 * NZ)
    xh = ctx // NY
    y = lax.rem(ctx, NY)
    x = xh * 2 + xl

    def at(xx=None, yy=None, zz=None, cc=None):
        xx = x if xx is None else xx
        yy = y if yy is None else yy
        zz = z if zz is None else zz
        cc = core if cc is None else cc
        return ((lax.rem(xx, 2) * NZ + zz) * 2 + cc, (xx // 2) * NY + yy)

    line = dp + 2 * NZ * (1 - 2 * xl)
    partner = (line, ctx)
    sibling = at(cc=1 - core)
    up = at(zz=lax.rem(z + 1, NZ))
    down = at(zz=lax.rem(z + NZ - 1, NZ))

    def peer(i):
        return lax.rem(xh + i // NY, 2) * NY + lax.rem(y + i % NY, NY)

    def send(src, dst, ssem, rsem, dev):
        pltpu.make_async_remote_copy(
            src_ref=src, dst_ref=dst, send_sem=ssem, recv_sem=rsem,
            device_id=dev, device_id_type=MESH,
        ).start()

    def local(src, dst, sem):
        pltpu.make_async_copy(src, dst, sem).start()

    def arrive(dst, sem):
        pltpu.make_async_copy(dst, dst, sem).wait()

    barrier = pltpu.get_barrier_semaphore()
    near = (1, 15, 2, 14, 3, 13, 4, 12)
    partners = [sibling]
    partners += [at(zz=lax.rem(z + i, NZ)) for i in near]
    partners += [(dp, peer(i)) for i in range(1, NCTX)]
    partners += [(line, peer(i)) for i in range(NCTX)]
    for dev in partners:
        pl.semaphore_signal(barrier, inc=1, device_id=dev, device_id_type=MESH)
    local(wg_ref.at[0], packed.at[0:176], l_s.at[0])
    local(wg_ref.at[1], packed.at[176:352], l_s.at[0])
    local(wd_ref, packed.at[352:528], l_s.at[0])
    local(res_ref, res, l_s.at[1])
    arrive(packed, l_s.at[0])
    pl.semaphore_wait(barrier, len(partners))

    other_rows = pl.ds(pl.multiple_of((1 - core) * HALF_STEP, 16), HALF)
    firsts = (lax.rem(z + 8, NZ), lax.rem(z + 9, NZ))
    for d in range(2):
        send(packed.at[other_rows, cols(firsts[d] * 128, 128)], early.at[d], early_s, early_r, sibling)
    send(packed.at[other_rows, :], oth, oth_s, oth_r, sibling)
    wo_part = wo_ref.at[:, cols(ctx * 256, 256)]
    for i in near:
        send(wo_part, wbuf.at[x, y, z, core], z_s.at[0], z_r.at[0], at(zz=lax.rem(z + i, NZ)))
    local(wo_part, wbuf.at[x, y, z, core], z_r.at[0])
    owners = (owner[0], owner[1])

    def weights():
        mate = dp + 1 - 2 * core
        own_rows = pl.ds(pl.multiple_of(core * HALF_STEP, 16), HALF)
        mine = [owners[e] == dp for e in range(2)]
        mates = [owners[e] == mate for e in range(2)]
        has = [jnp.logical_or(mine[e], mates[e]) for e in range(2)]

        def pick(e, a, b):
            return lax.select(mine[e], a, lax.select(mates[e], b, jnp.zeros_like(b)))

        to = (up, down)
        arrive(early, early_r)
        for d in range(2):
            a = packed[own_rows, cols(firsts[d] * 128, 128)]
            for e in range(2):
                lead[e, d] = pick(e, a, early[d])
                for h in range(2):
                    dst = rsb.at[e, HOPS * d, span(h)]
                    send(lead.at[e, d, span(h)], dst, rs_s, rs_r.at[e, HOPS * d, h], to[d])
        yield
        arrive(oth, oth_r)
        for c in range(NZ):
            a = packed[own_rows, c * 128:(c + 1) * 128]
            b = oth[:, c * 128:(c + 1) * 128]
            for e in range(2):
                cand[e, c] = pick(e, a, b)
        for t in range(HOPS):
            for d in range(2):
                last = HOPS - 1 - d
                if t > last:
                    continue
                slot = HOPS * d + t
                c = lax.rem(z + 7 - t, NZ) if d == 0 else lax.rem(z + 10 + t, NZ)
                for e in range(2):
                    for h in range(2):
                        got = rsb.at[e, slot, span(h)]
                        arrive(got, rs_r.at[e, slot, h])
                        if t < last:
                            got[...] = lax.select(has[e], cand[e, c, span(h)], got[...])
                            send(got, rsb.at[e, slot + 1, span(h)], rs_s, rs_r.at[e, slot + 1, h], to[d])
            yield

        def settled(e, known):
            met = rsb[e, HOPS - 1] + rsb[e, 2 * HOPS - 2]
            return lax.select(known, cand[e, z], met)

        known = jnp.where(xl == 0, has[1].astype(jnp.int32), has[0].astype(jnp.int32)) > 0
        xsend[...] = settled(1 - xl, known)
        send(xsend, xpiece, xp_s, xp_r, partner)
        known = jnp.where(xl == 0, has[0].astype(jnp.int32), has[1].astype(jnp.int32)) > 0
        here = settled(xl, known)
        arrive(xpiece, xp_r)
        wf[core, :, cols(z * 128, 128)] = here + xpiece[...]

        def piece(c):
            return wf.at[core, :, cols(c * 128, 128)]

        far = (at(zz=lax.rem(z + 2, NZ)), at(zz=lax.rem(z + NZ - 2, NZ)))

        def onward(c, d, t):
            if t < HOPS // 2 - d:
                send(piece(c), piece(c), ag_s.at[0], ag_r.at[d, 2 * t + 1], far[d])
            if t < HOPS // 2:
                send(piece(c), piece(c), ag_s.at[1], ag_r.at[d, 2 * t], to[d])
            send(piece(c), piece(c), cc_s, cc_r, sibling)

        def source(d, hops):
            return lax.rem(z + (NZ - hops if d == 0 else hops), NZ)

        for d in range(2):
            send(piece(z), piece(z), ag_s.at[0], ag_r.at[d, 1], far[d])
        for d in range(2):
            send(piece(z), piece(z), ag_s.at[1], ag_r.at[d, 0], to[d])
        send(piece(z), piece(z), cc_s, cc_r, sibling)
        yield
        for t in range(1, HOPS // 2 + 1):
            for d in range(2):
                if t <= HOPS // 2 - d:
                    c = source(d, 2 * t)
                    arrive(piece(c), ag_r.at[d, 2 * t - 1])
                    onward(c, d, t)
            yield
            for d in range(2):
                c = source(d, 2 * t - 1)
                arrive(piece(c), ag_r.at[d, 2 * t - 2])
                send(piece(c), piece(c), cc_s, cc_r, sibling)
            yield

    def a_slab(yy):
        return wbuf.at[:, yy, pl.ds(0, 8), core]

    def b_slab(xx):
        return wbuf.at[xx, :, pl.ds(8, 8), core]

    def main():
        for i in range(1, NCTX):
            for j, ref in enumerate((q_ref, k_ref, v_ref)):
                send(ref.at[:, cols(peer(i) * HD, HD)], qkv.at[j, ctx], q_s, q_r.at[ctx], (dp, peer(i)))
        for j, ref in enumerate((q_ref, k_ref, v_ref)):
            local(ref.at[:, cols(ctx * HD, HD)], qkv.at[j, ctx], q_r.at[ctx])
        yield
        arrive(wbuf.at[0, 0, pl.ds(0, 9), 0], z_r.at[0])
        for i in (1, 2, 3, 4):
            block = wbuf.at[x, y, lax.rem(z + NZ - i, NZ), core]
            send(block, block, z_s.at[1], z_r.at[1], at(zz=lax.rem(z + 4, NZ)))
            if i < 4:
                block = wbuf.at[x, y, lax.rem(z + i, NZ), core]
                send(block, block, z_s.at[1], z_r.at[1], at(zz=lax.rem(z + 12, NZ)))
        yield
        arrive(wbuf.at[0, 0, pl.ds(0, 7), 0], z_r.at[1])
        a_own = wbuf.at[x, y, pl.ds(0, 8), core]
        b_own = wbuf.at[x, y, pl.ds(8, 8), core]
        for i in range(1, 4):
            send(a_own, a_own, p1_s, p1_r.at[0], at(xx=lax.rem(x + i, NX)))
            send(b_own, b_own, p1_s, p1_r.at[1], at(yy=lax.rem(y + i, NY)))
        yield
        three = wbuf.at[pl.ds(0, 3), 0, pl.ds(0, 8), 0]
        arrive(three, p1_r.at[0])
        arrive(three, p1_r.at[1])
        for i in (1, 3, 2):
            send(a_slab(y), a_slab(y), p2_s, p2_r.at[0, y], at(yy=lax.rem(y + i, NY)))
            send(b_slab(x), b_slab(x), p2_s, p2_r.at[1, x], at(xx=lax.rem(x + i, NX)))
            yield
        send(a_slab(y), a_slab(y), c_s, c_r, sibling)
        send(b_slab(x), b_slab(x), c_s, c_r, sibling)
        yield
        for b in range(4):
            for i in (2 * b, 2 * b + 1):
                arrive(qkv.at[:, i], q_r.at[i])
            n = (b + 1) * 256
            q = qkv[0, 2 * b:2 * b + 2].reshape(256, HD)
            k = qkv[1, : 2 * b + 2].reshape(n, HD)
            v = qkv[2, : 2 * b + 2].reshape(n, HD)
            s = dot(q, k, NT) * HD ** (-0.5)
            qpos = lax.broadcasted_iota(jnp.int32, (256, n), 0) + b * 256
            kpos = lax.broadcasted_iota(jnp.int32, (256, n), 1)
            s = jnp.where(kpos <= qpos, s, -jnp.inf)
            w = jnp.exp(s - jnp.max(s, axis=1, keepdims=True))
            total = jnp.sum(w, axis=1, keepdims=True)
            o = dot(w.astype(BF), v) / total
            abuf[2 * b:2 * b + 2] = o.astype(BF).reshape(2, 128, HD)
            yield
        mine = attd.at[:, cols(ctx * HD, HD)]
        for i in range(1, NCTX):
            send(abuf.at[peer(i)], mine, a_s, a_r, (dp, peer(i)))
        local(abuf.at[ctx], mine, a_r)
        yield
        for i in (1, 3, 2):
            xx, yy = lax.rem(x + i, NX), lax.rem(y + i, NY)
            arrive(a_slab(yy), p2_r.at[0, yy])
            send(a_slab(yy), a_slab(yy), c_s, c_r, sibling)
            arrive(b_slab(xx), p2_r.at[1, xx])
            send(b_slab(xx), b_slab(xx), c_s, c_r, sibling)
            yield
        arrive(attd, a_r)
        arrive(res, l_s.at[1])
        arrive(wbuf.at[:, :, :, 1 - core], c_r)
        squares = jnp.zeros((TOK, 1), F32)
        for i in range(NCTX):
            acc = dot(attd[:, :512], wbuf[(i // NY) * 2, i % NY].reshape(512, 256))
            acc += dot(attd[:, 512:], wbuf[(i // NY) * 2 + 1, i % NY].reshape(512, 256))
            out = acc.astype(BF)
            here = slice(i * 256, (i + 1) * 256)
            proj_ref[:, here] = out
            combined = res[:, here].astype(F32) + out.astype(F32)
            squares += jnp.sum(combined * combined, axis=1, keepdims=True)
            if i % 4 == 3:
                yield
        scale = lax.rsqrt(squares * (1.0 / D) + EPSILON)
        for i in range(NCTX):
            here = slice(i * 256, (i + 1) * 256)
            combined = res[:, here].astype(F32) + proj_ref[:, here].astype(F32)
            normed[:, here] = (combined * scale * gain_ref[:, here]).astype(BF)
        for e, dst in ((xl, rbuf.at[xl, ctx]), (1 - xl, dsend)):
            first, second = slot_rows(ids_ref, jnp.where(e == 0, caps[0], caps[1]), e)
            rows = dot(first.astype(BF), normed[:, :1024]) + dot(second.astype(BF), normed[:, 1024:])
            dst[...] = rows.astype(BF)
        slot = rbuf.at[xl, ctx]
        for i in (2, 6, 3, 7, 1, 5, 4, 0):
            group = 0 if i % NY >= 2 else 1
            if i:
                send(slot, slot, r_s.at[0], r_r.at[group], (dp, peer(i)))
            send(dsend, slot, r_s.at[1], r_r.at[group], (line, peer(i)))
            yield

    threads = {"w": weights(), "m": main()}
    for step in SCHEDULE:
        next(threads[step], 0)
    for step in ("m", "w"):
        for _ in threads[step]:
            pass

    arrive(wf.at[1 - core], cc_r)
    uw[0:80] = wf[0, 176:256]
    uw[80:176] = wf[1, 0:96]
    for g, group in enumerate(GROUPS):
        arrive(rbuf.at[0, pl.ds(0, 8 - g)], r_r.at[g])
        r = jnp.concatenate(
            [rbuf[s, peer(i)] for i in group for s in (xl, 1 - xl)], axis=0
        )
        pair = []
        for w in (wf.at[0, 0:176], uw):
            left = dot(r, w[:, :1024], NT).reshape(8, 48, FF_DEV)
            right = dot(r, w[:, 1024:], NT).reshape(8, 48, FF_DEV)
            pair.append((left[:, :CAP] + right[:, CAP:]).reshape(8 * CAP, FF_DEV))
        gate_proj, up_proj = pair
        hidden = (gate_proj / (1.0 + jnp.exp(-gate_proj)) * up_proj).astype(BF)
        halves = [
            dot(hidden, wf[1, 96:272, h * 1024:(h + 1) * 1024]).reshape(8, CAP, 1024)
            for h in range(2)
        ]
        out = jnp.concatenate(halves, axis=1).astype(BF)
        for j, i in enumerate(group):
            for s in range(2):
                xx = lax.rem(xh + i // NY, 2) * 2 + (xl if s == 0 else 1 - xl)
                for h in range(2):
                    sbuf[h, xx, lax.rem(y + i % NY, NY)] = out[2 * j + s, :, h * 512:(h + 1) * 512]
        for i in ((1, 2), (3,))[g]:
            yy = lax.rem(y + i, NY)
            send(sbuf.at[0, :, yy], a1.at[y], e_s.at[0], e_r.at[0], at(yy=yy))

    across = [lax.rem(x + i, NX) for i in range(NX)]
    along = [lax.rem(y + i, NY) for i in range(NY)]
    for i in (1, 3, 2):
        send(sbuf.at[1, across[i]], b1.at[x], e_s.at[1], e_r.at[1], at(xx=across[i]))

    def wide(*parts):
        acc = parts[0].astype(F32)
        for part in parts[1:]:
            acc += part.astype(F32)
        return acc.astype(BF)

    arrive(a1.at[pl.ds(0, 3)], e_r.at[0])
    for i in (2, 1, 3, 0):
        xx = across[i]
        sa[xx] = wide(sbuf[0, xx, y], *[a1[along[j], xx] for j in range(1, NY)])
        if i:
            send(sa.at[xx], a2.at[x], e_s.at[2], e_r.at[2], at(xx=xx))
    arrive(b1.at[pl.ds(0, 3)], e_r.at[1])
    for i in (2, 1, 3, 0):
        yy = along[i]
        sb[yy, 0] = wide(sbuf[1, x, yy], b1[across[2], yy])
        sb[yy, 1] = wide(b1[across[1], yy], b1[across[3], yy])
        if i:
            send(sb.at[yy], b2.at[y], e_s.at[3], e_r.at[3], at(yy=yy))
    arrive(a2.at[pl.ds(0, 3)], e_r.at[2])
    tot_ref[xl, :, :512] = wide(sa[x], a2[across[2]])
    tot_ref[1 - xl, :, :512] = wide(a2[across[1]], a2[across[3]])
    arrive(b2.at[pl.ds(0, 3)], e_r.at[3])
    for s, e in ((0, xl), (1, 1 - xl)):
        tot_ref[e, :, 512:] = wide(sb[y, s], *[b2[along[j], s] for j in range(1, NY)])

    arrive(early, early_s)
    arrive(oth, oth_s)
    arrive(wbuf.at[0, 0, pl.ds(0, 8), 0], z_s.at[0])
    arrive(wbuf.at[0, 0, pl.ds(0, 7), 0], z_s.at[1])
    arrive(qkv.at[:, pl.ds(0, NCTX - 1)], q_s)
    arrive(abuf.at[pl.ds(0, NCTX - 1)], a_s)
    arrive(wbuf.at[pl.ds(0, 3), pl.ds(0, 2), pl.ds(0, 8), 0], p1_s)
    arrive(wbuf.at[pl.ds(0, 3), :, :, 0], p2_s)
    arrive(wbuf.at[:, :, :, 0], c_s)
    arrive(rsb, rs_s)
    arrive(xsend, xp_s)
    arrive(wf.at[0, :, pl.ds(0, 7 * 128)], ag_s.at[0])
    arrive(wf.at[0, :, pl.ds(0, 8 * 128)], ag_s.at[1])
    arrive(wf.at[0], cc_s)
    arrive(rbuf.at[0, pl.ds(0, 7)], r_s.at[0])
    arrive(rbuf.at[0], r_s.at[1])
    for i, buf in enumerate((a1, b1, a2, b2)):
        arrive(buf.at[pl.ds(0, 3)], e_s.at[i])


def combine(caps, ids_ref, gates_ref, tot_ref, proj_ref, out_ref, sum_ref):
    out_ref[...] = proj_ref[...]
    firsts, seconds, rows = [], [], []
    for e in range(2):
        gate = jnp.zeros((1, TOK), F32)
        for i in range(PICKS):
            gate += jnp.where(ids_ref[i] == e, gates_ref[i], 0.0)
        high = gate.astype(BF).astype(F32)
        first, second = slot_rows(ids_ref, caps[e], e)
        for g in (high, gate - high):
            firsts.append(first * g)
            seconds.append(second * g)
            rows.append(tot_ref[e])
    rows = jnp.concatenate(rows, axis=0)
    sum_ref[:, :1024] = dot(jnp.concatenate(firsts, axis=0).astype(BF), rows, TN).astype(BF)
    sum_ref[:, 1024:] = dot(jnp.concatenate(seconds, axis=0).astype(BF), rows, TN).astype(BF)


def body(
    query_vecs, key_vecs, value_vecs, residual, w_out, norm_gain, w_gate_up,
    w_down, expert_ids, route_gates, capacity, expert_owner,
):
    hbm = pl.BlockSpec(memory_space=pl.ANY)
    vmem = pl.BlockSpec(memory_space=pltpu.VMEM)
    smem = pl.BlockSpec(memory_space=pltpu.SMEM)
    dma = pltpu.SemaphoreType.DMA
    out = jax.ShapeDtypeStruct((TOK, D), BF)
    rows = (2 * CAP, 1024)
    half = (2 * CAP, 512)
    ids = jnp.transpose(expert_ids, (2, 0, 1))
    gates = jnp.transpose(route_gates, (2, 0, 1))
    proj, tot = pl.pallas_call(
        kernel,
        out_shape=(out, jax.ShapeDtypeStruct((2,) + rows, BF)),
        in_specs=[smem, smem] + [hbm] * 7 + [vmem] * 2,
        out_specs=(vmem, vmem),
        scratch_shapes=[
            pltpu.VMEM((3, NCTX, TOK, HD), BF),
            pltpu.VMEM((NCTX, TOK, HD), BF),
            pltpu.VMEM((TOK, NCTX * HD), BF),
            pltpu.VMEM((NX, NY, NZ, 2, 16, 256), BF),
            pltpu.VMEM((TOK, D), BF),
            pltpu.VMEM((3 * FF_DEV, D), BF),
            pltpu.VMEM((2, HALF, 128), BF),
            pltpu.VMEM((2, 2, HALF, 128), BF),
            pltpu.VMEM((HALF, D), BF),
            pltpu.VMEM((2, NZ, HALF, 128), BF),
            pltpu.VMEM((2, NZ - 1, HALF, 128), BF),
            pltpu.VMEM((HALF, 128), BF),
            pltpu.VMEM((HALF, 128), BF),
            pltpu.VMEM((2, HALF, D), BF),
            pltpu.VMEM((FF_DEV, D), BF),
            pltpu.VMEM((TOK, D), BF),
            pltpu.VMEM((2, NCTX) + rows, BF),
            pltpu.VMEM(rows, BF),
            pltpu.VMEM((2, NX, NY) + half, BF),
            pltpu.VMEM((NY, NX) + half, BF),
            pltpu.VMEM((NX, NY) + half, BF),
            pltpu.VMEM((NX,) + half, BF),
            pltpu.VMEM((NY, 2) + half, BF),
            pltpu.VMEM((NX,) + half, BF),
            pltpu.VMEM((NY, 2) + half, BF),
            dma, dma((NCTX,)), dma, dma, dma((2,)), dma((2,)),
            dma, dma((2,)), dma, dma((2, 4)), dma, dma,
            dma((2,)), dma, dma, dma, dma, dma, dma((2, NZ - 1, 2)), dma, dma,
            dma((2,)), dma((2, HOPS)), dma, dma,
            dma((2,)), dma((2,)), dma((4,)), dma((4,)),
        ],
        compiler_params=pltpu.CompilerParams(
            collective_id=0, has_side_effects=True, vmem_limit_bytes=58 << 20
        ),
    )(
        expert_owner[:2], capacity[0, 0],
        query_vecs[0], key_vecs[0], value_vecs[0], residual[0], w_out,
        jnp.swapaxes(w_gate_up[0], 1, 2), w_down[0], norm_gain[None], ids,
    )
    attn_proj, expert_sum = pl.pallas_call(
        combine,
        out_shape=(out, out),
        in_specs=[smem] + [vmem] * 4,
        out_specs=(vmem, vmem),
    )(capacity[0, 0], ids, gates, tot, proj)
    return (attn_proj[None], expert_sum[None])


def solution(mesh):
    seq = P("dp", "ctx", None)
    placed = (
        seq, seq, seq, seq, P("dp", None), P(),
        P("dp", None, None, "ctx"), seq, seq, seq, seq, P(),
    )
    return jax.shard_map(
        body, mesh=mesh, in_specs=placed, out_specs=(seq, seq), check_vma=False
    )
```

```python
import jax
import jax.numpy as jnp
from jax import lax
from jax.experimental import pallas as pl
from jax.experimental.pallas import tpu as pltpu
from jax.sharding import PartitionSpec as P

D = 2048
HD = 128
FF_DEV = 176
CAP = 24
TOK = 128
PICKS = 6
NZ = 16
NY = 4
NX = 4
NCTX = 8
HALF = 272
HALF_STEP = 256
HOPS = NZ // 2
EPSILON = 1e-06
MESH = pl.DeviceIdType.MESH
BF = jnp.bfloat16
F32 = jnp.float32

NN = (((1,), (0,)), ((), ()))
NT = (((1,), (1,)), ((), ()))
TN = (((0,), (0,)), ((), ()))

SCHEDULE = "mwmwmwmwmwmmmmwmmmwmwmwmwmwmmwmwmwmwmwmwmwmw"
GROUPS = ((1, 2, 5, 6), (3, 0, 7, 4))
PARTS = ((0, 144), (144, 128))


def dot(a, b, dims=NN):
    return lax.dot_general(a, b, dims, preferred_element_type=F32)


def span(h):
    return pl.ds(*PARTS[h])


def cols(start, size):
    return pl.ds(pl.multiple_of(start, 128), size)


def slot_rows(ids_ref, cap, e):
    routed = jnp.zeros((1, TOK), F32)
    for i in range(PICKS):
        routed += jnp.where(ids_ref[i] == e, 1.0, 0.0)
    rows = lax.broadcasted_iota(jnp.int32, (TOK, TOK), 0)
    lanes = lax.broadcasted_iota(jnp.int32, (TOK, TOK), 1)
    before = jnp.where(rows < lanes, 1.0, 0.0).astype(BF)
    rank = dot(jnp.broadcast_to(routed, (8, TOK)).astype(BF), before)[0:1]
    kept = jnp.where(rank < cap.astype(F32), routed, 0.0)
    rank = jnp.where(kept > 0.5, rank, -1000.0)
    slot = lax.broadcasted_iota(jnp.int32, (2 * CAP, TOK), 0).astype(F32)
    first = jnp.where(rank == slot, 1.0, 0.0)
    second = jnp.where(rank == slot - CAP, 1.0, 0.0)
    return first, second


def kernel(
    owner, caps,
    q_ref, k_ref, v_ref, res_ref, wo_ref, wg_ref, wd_ref, gain_ref, ids_ref,
    proj_ref, tot_ref,
    qkv, abuf, attd, wbuf, res, packed, early, lead, oth, cand, rsb, xsend, xpiece, wf, uw,
    normed, rbuf, dsend, sbuf, a1, b1, sa, sb, a2, b2,
    q_s, q_r, a_s, a_r, z_s, z_r, p1_s, p1_r, p2_s, p2_r, c_s, c_r,
    l_s, early_s, early_r, oth_s, oth_r, rs_s, rs_r, xp_s, xp_r, ag_s, ag_r, cc_s, cc_r,
    r_s, r_r, e_s, e_r,
):
    dp = lax.axis_index("dp")
    ctx = lax.axis_index("ctx")
    core = lax.rem(dp, 2)
    z = lax.rem(dp // 2, NZ)
    xl = dp // (2 * NZ)
    xh = ctx // NY
    y = lax.rem(ctx, NY)
    x = xh * 2 + xl

    def at(xx=None, yy=None, zz=None, cc=None):
        xx = x if xx is None else xx
        yy = y if yy is None else yy
        zz = z if zz is None else zz
        cc = core if cc is None else cc
        return ((lax.rem(xx, 2) * NZ + zz) * 2 + cc, (xx // 2) * NY + yy)

    line = dp + 2 * NZ * (1 - 2 * xl)
    partner = (line, ctx)
    sibling = at(cc=1 - core)
    up = at(zz=lax.rem(z + 1, NZ))
    down = at(zz=lax.rem(z + NZ - 1, NZ))

    def peer(i):
        return lax.rem(xh + i // NY, 2) * NY + lax.rem(y + i % NY, NY)

    def send(src, dst, ssem, rsem, dev):
        pltpu.make_async_remote_copy(
            src_ref=src, dst_ref=dst, send_sem=ssem, recv_sem=rsem,
            device_id=dev, device_id_type=MESH,
        ).start()

    def local(src, dst, sem):
        pltpu.make_async_copy(src, dst, sem).start()

    def arrive(dst, sem):
        pltpu.make_async_copy(dst, dst, sem).wait()

    barrier = pltpu.get_barrier_semaphore()
    near = (1, 15, 2, 14, 3, 13, 4, 12)
    partners = [sibling]
    partners += [at(zz=lax.rem(z + i, NZ)) for i in near]
    partners += [(dp, peer(i)) for i in range(1, NCTX)]
    partners += [(line, peer(i)) for i in range(NCTX)]
    for dev in partners:
        pl.semaphore_signal(barrier, inc=1, device_id=dev, device_id_type=MESH)
    local(wg_ref.at[0], packed.at[0:176], l_s.at[0])
    local(wg_ref.at[1], packed.at[176:352], l_s.at[0])
    local(wd_ref, packed.at[352:528], l_s.at[0])
    local(res_ref, res, l_s.at[1])
    arrive(packed, l_s.at[0])
    pl.semaphore_wait(barrier, len(partners))

    other_rows = pl.ds(pl.multiple_of((1 - core) * HALF_STEP, 16), HALF)
    firsts = (lax.rem(z + 8, NZ), lax.rem(z + 9, NZ))
    for d in range(2):
        send(packed.at[other_rows, cols(firsts[d] * 128, 128)], early.at[d], early_s, early_r, sibling)
    send(packed.at[other_rows, :], oth, oth_s, oth_r, sibling)
    wo_part = wo_ref.at[:, cols(ctx * 256, 256)]
    for i in near:
        send(wo_part, wbuf.at[x, y, z, core], z_s.at[0], z_r.at[0], at(zz=lax.rem(z + i, NZ)))
    local(wo_part, wbuf.at[x, y, z, core], z_r.at[0])
    owners = (owner[0], owner[1])

    def weights():
        mate = dp + 1 - 2 * core
        own_rows = pl.ds(pl.multiple_of(core * HALF_STEP, 16), HALF)
        mine = [owners[e] == dp for e in range(2)]
        mates = [owners[e] == mate for e in range(2)]
        has = [jnp.logical_or(mine[e], mates[e]) for e in range(2)]

        def pick(e, a, b):
            return lax.select(mine[e], a, lax.select(mates[e], b, jnp.zeros_like(b)))

        to = (up, down)
        arrive(early, early_r)
        for d in range(2):
            a = packed[own_rows, cols(firsts[d] * 128, 128)]
            for e in range(2):
                lead[e, d] = pick(e, a, early[d])
                for h in range(2):
                    dst = rsb.at[e, HOPS * d, span(h)]
                    send(lead.at[e, d, span(h)], dst, rs_s, rs_r.at[e, HOPS * d, h], to[d])
        yield
        arrive(oth, oth_r)
        for c in range(NZ):
            a = packed[own_rows, c * 128:(c + 1) * 128]
            b = oth[:, c * 128:(c + 1) * 128]
            for e in range(2):
                cand[e, c] = pick(e, a, b)
        for t in range(HOPS):
            for d in range(2):
                last = HOPS - 1 - d
                if t > last:
                    continue
                slot = HOPS * d + t
                c = lax.rem(z + 7 - t, NZ) if d == 0 else lax.rem(z + 10 + t, NZ)
                for e in range(2):
                    for h in range(2):
                        got = rsb.at[e, slot, span(h)]
                        arrive(got, rs_r.at[e, slot, h])
                        if t < last:
                            got[...] = lax.select(has[e], cand[e, c, span(h)], got[...])
                            send(got, rsb.at[e, slot + 1, span(h)], rs_s, rs_r.at[e, slot + 1, h], to[d])
            yield

        def settled(e, known):
            met = rsb[e, HOPS - 1] + rsb[e, 2 * HOPS - 2]
            return lax.select(known, cand[e, z], met)

        known = jnp.where(xl == 0, has[1].astype(jnp.int32), has[0].astype(jnp.int32)) > 0
        xsend[...] = settled(1 - xl, known)
        send(xsend, xpiece, xp_s, xp_r, partner)
        yield
        known = jnp.where(xl == 0, has[0].astype(jnp.int32), has[1].astype(jnp.int32)) > 0
        here = settled(xl, known)
        arrive(xpiece, xp_r)
        wf[core, :, cols(z * 128, 128)] = here + xpiece[...]

        def piece(c):
            return wf.at[core, :, cols(c * 128, 128)]

        far = (at(zz=lax.rem(z + 2, NZ)), at(zz=lax.rem(z + NZ - 2, NZ)))

        def onward(c, d, t):
            if t < HOPS // 2 - d:
                send(piece(c), piece(c), ag_s.at[0], ag_r.at[d, 2 * t + 1], far[d])
            if t < HOPS // 2:
                send(piece(c), piece(c), ag_s.at[1], ag_r.at[d, 2 * t], to[d])
            send(piece(c), piece(c), cc_s, cc_r, sibling)

        def source(d, hops):
            return lax.rem(z + (NZ - hops if d == 0 else hops), NZ)

        for d in range(2):
            send(piece(z), piece(z), ag_s.at[0], ag_r.at[d, 1], far[d])
        for d in range(2):
            send(piece(z), piece(z), ag_s.at[1], ag_r.at[d, 0], to[d])
        send(piece(z), piece(z), cc_s, cc_r, sibling)
        yield
        for t in range(1, HOPS // 2 + 1):
            for d in range(2):
                if t <= HOPS // 2 - d:
                    c = source(d, 2 * t)
                    arrive(piece(c), ag_r.at[d, 2 * t - 1])
                    onward(c, d, t)
            yield
            for d in range(2):
                c = source(d, 2 * t - 1)
                arrive(piece(c), ag_r.at[d, 2 * t - 2])
                send(piece(c), piece(c), cc_s, cc_r, sibling)
            yield

    def a_slab(yy):
        return wbuf.at[:, yy, pl.ds(0, 8), core]

    def b_slab(xx):
        return wbuf.at[xx, :, pl.ds(8, 8), core]

    def main():
        for i in range(1, NCTX):
            for j, ref in enumerate((q_ref, k_ref, v_ref)):
                send(ref.at[:, cols(peer(i) * HD, HD)], qkv.at[j, ctx], q_s, q_r.at[ctx], (dp, peer(i)))
        for j, ref in enumerate((q_ref, k_ref, v_ref)):
            local(ref.at[:, cols(ctx * HD, HD)], qkv.at[j, ctx], q_r.at[ctx])
        yield
        arrive(wbuf.at[0, 0, pl.ds(0, 9), 0], z_r.at[0])
        for i in (1, 2, 3, 4):
            block = wbuf.at[x, y, lax.rem(z + NZ - i, NZ), core]
            send(block, block, z_s.at[1], z_r.at[1], at(zz=lax.rem(z + 4, NZ)))
            if i < 4:
                block = wbuf.at[x, y, lax.rem(z + i, NZ), core]
                send(block, block, z_s.at[1], z_r.at[1], at(zz=lax.rem(z + 12, NZ)))
        yield
        arrive(wbuf.at[0, 0, pl.ds(0, 7), 0], z_r.at[1])
        a_own = wbuf.at[x, y, pl.ds(0, 8), core]
        b_own = wbuf.at[x, y, pl.ds(8, 8), core]
        for i in range(1, 4):
            send(a_own, a_own, p1_s, p1_r.at[0], at(xx=lax.rem(x + i, NX)))
            send(b_own, b_own, p1_s, p1_r.at[1], at(yy=lax.rem(y + i, NY)))
        yield
        three = wbuf.at[pl.ds(0, 3), 0, pl.ds(0, 8), 0]
        arrive(three, p1_r.at[0])
        arrive(three, p1_r.at[1])
        for i in (1, 3, 2):
            send(a_slab(y), a_slab(y), p2_s, p2_r.at[0, y], at(yy=lax.rem(y + i, NY)))
            send(b_slab(x), b_slab(x), p2_s, p2_r.at[1, x], at(xx=lax.rem(x + i, NX)))
            yield
        send(a_slab(y), a_slab(y), c_s, c_r, sibling)
        send(b_slab(x), b_slab(x), c_s, c_r, sibling)
        yield
        for b in range(4):
            for i in (2 * b, 2 * b + 1):
                arrive(qkv.at[:, i], q_r.at[i])
            n = (b + 1) * 256
            q = qkv[0, 2 * b:2 * b + 2].reshape(256, HD)
            k = qkv[1, : 2 * b + 2].reshape(n, HD)
            v = qkv[2, : 2 * b + 2].reshape(n, HD)
            s = dot(q, k, NT) * HD ** (-0.5)
            qpos = lax.broadcasted_iota(jnp.int32, (256, n), 0) + b * 256
            kpos = lax.broadcasted_iota(jnp.int32, (256, n), 1)
            s = jnp.where(kpos <= qpos, s, -jnp.inf)
            w = jnp.exp(s - jnp.max(s, axis=1, keepdims=True))
            total = jnp.sum(w, axis=1, keepdims=True)
            o = dot(w.astype(BF), v) / total
            abuf[2 * b:2 * b + 2] = o.astype(BF).reshape(2, 128, HD)
            yield
        mine = attd.at[:, cols(ctx * HD, HD)]
        for i in range(1, NCTX):
            send(abuf.at[peer(i)], mine, a_s, a_r, (dp, peer(i)))
        local(abuf.at[ctx], mine, a_r)
        yield
        for i in (1, 3, 2):
            xx, yy = lax.rem(x + i, NX), lax.rem(y + i, NY)
            arrive(a_slab(yy), p2_r.at[0, yy])
            send(a_slab(yy), a_slab(yy), c_s, c_r, sibling)
            arrive(b_slab(xx), p2_r.at[1, xx])
            send(b_slab(xx), b_slab(xx), c_s, c_r, sibling)
            yield
        arrive(attd, a_r)
        arrive(res, l_s.at[1])
        arrive(wbuf.at[:, :, :, 1 - core], c_r)
        squares = jnp.zeros((TOK, 1), F32)
        for i in range(NCTX):
            acc = dot(attd[:, :512], wbuf[(i // NY) * 2, i % NY].reshape(512, 256))
            acc += dot(attd[:, 512:], wbuf[(i // NY) * 2 + 1, i % NY].reshape(512, 256))
            out = acc.astype(BF)
            here = slice(i * 256, (i + 1) * 256)
            proj_ref[:, here] = out
            combined = res[:, here].astype(F32) + out.astype(F32)
            squares += jnp.sum(combined * combined, axis=1, keepdims=True)
            if i % 4 == 3:
                yield
        scale = lax.rsqrt(squares * (1.0 / D) + EPSILON)
        for i in range(NCTX):
            here = slice(i * 256, (i + 1) * 256)
            combined = res[:, here].astype(F32) + proj_ref[:, here].astype(F32)
            normed[:, here] = (combined * scale * gain_ref[:, here]).astype(BF)
        for e, dst in ((xl, rbuf.at[xl, ctx]), (1 - xl, dsend)):
            first, second = slot_rows(ids_ref, jnp.where(e == 0, caps[0], caps[1]), e)
            rows = dot(first.astype(BF), normed[:, :1024]) + dot(second.astype(BF), normed[:, 1024:])
            dst[...] = rows.astype(BF)
        slot = rbuf.at[xl, ctx]
        for i in (2, 6, 3, 7, 1, 5, 4, 0):
            group = 0 if i % NY >= 2 else 1
            if i:
                send(slot, slot, r_s.at[0], r_r.at[group], (dp, peer(i)))
            send(dsend, slot, r_s.at[1], r_r.at[group], (line, peer(i)))
            yield

    threads = {"w": weights(), "m": main()}
    for step in SCHEDULE:
        next(threads[step], 0)
    for step in ("m", "w"):
        for _ in threads[step]:
            pass

    arrive(wf.at[1 - core], cc_r)
    uw[0:80] = wf[0, 176:256]
    uw[80:176] = wf[1, 0:96]
    for g, group in enumerate(GROUPS):
        arrive(rbuf.at[0, pl.ds(0, 8 - g)], r_r.at[g])
        r = jnp.concatenate(
            [rbuf[s, peer(i)] for i in group for s in (xl, 1 - xl)], axis=0
        )
        pair = []
        for w in (wf.at[0, 0:176], uw):
            left = dot(r, w[:, :1024], NT).reshape(8, 48, FF_DEV)
            right = dot(r, w[:, 1024:], NT).reshape(8, 48, FF_DEV)
            pair.append((left[:, :CAP] + right[:, CAP:]).reshape(8 * CAP, FF_DEV))
        gate_proj, up_proj = pair
        hidden = (gate_proj / (1.0 + jnp.exp(-gate_proj)) * up_proj).astype(BF)
        halves = [
            dot(hidden, wf[1, 96:272, h * 1024:(h + 1) * 1024]).reshape(8, CAP, 1024)
            for h in range(2)
        ]
        out = jnp.concatenate(halves, axis=1).astype(BF)
        for j, i in enumerate(group):
            for s in range(2):
                xx = lax.rem(xh + i // NY, 2) * 2 + (xl if s == 0 else 1 - xl)
                for h in range(2):
                    sbuf[h, xx, lax.rem(y + i % NY, NY)] = out[2 * j + s, :, h * 512:(h + 1) * 512]
        for i in ((1, 2), (3,))[g]:
            yy = lax.rem(y + i, NY)
            send(sbuf.at[0, :, yy], a1.at[y], e_s.at[0], e_r.at[0], at(yy=yy))

    across = [lax.rem(x + i, NX) for i in range(NX)]
    along = [lax.rem(y + i, NY) for i in range(NY)]
    for i in (1, 3, 2):
        send(sbuf.at[1, across[i]], b1.at[x], e_s.at[1], e_r.at[1], at(xx=across[i]))

    def wide(*parts):
        acc = parts[0].astype(F32)
        for part in parts[1:]:
            acc += part.astype(F32)
        return acc.astype(BF)

    arrive(a1.at[pl.ds(0, 3)], e_r.at[0])
    for i in (2, 1, 3, 0):
        xx = across[i]
        sa[xx] = wide(sbuf[0, xx, y], *[a1[along[j], xx] for j in range(1, NY)])
        if i:
            send(sa.at[xx], a2.at[x], e_s.at[2], e_r.at[2], at(xx=xx))
    arrive(b1.at[pl.ds(0, 3)], e_r.at[1])
    for i in (2, 1, 3, 0):
        yy = along[i]
        sb[yy, 0] = wide(sbuf[1, x, yy], b1[across[2], yy])
        sb[yy, 1] = wide(b1[across[1], yy], b1[across[3], yy])
        if i:
            send(sb.at[yy], b2.at[y], e_s.at[3], e_r.at[3], at(yy=yy))
    arrive(a2.at[pl.ds(0, 3)], e_r.at[2])
    tot_ref[xl, :, :512] = wide(sa[x], a2[across[2]])
    tot_ref[1 - xl, :, :512] = wide(a2[across[1]], a2[across[3]])
    arrive(b2.at[pl.ds(0, 3)], e_r.at[3])
    for s, e in ((0, xl), (1, 1 - xl)):
        tot_ref[e, :, 512:] = wide(sb[y, s], *[b2[along[j], s] for j in range(1, NY)])

    arrive(early, early_s)
    arrive(oth, oth_s)
    arrive(wbuf.at[0, 0, pl.ds(0, 8), 0], z_s.at[0])
    arrive(wbuf.at[0, 0, pl.ds(0, 7), 0], z_s.at[1])
    arrive(qkv.at[:, pl.ds(0, NCTX - 1)], q_s)
    arrive(abuf.at[pl.ds(0, NCTX - 1)], a_s)
    arrive(wbuf.at[pl.ds(0, 3), pl.ds(0, 2), pl.ds(0, 8), 0], p1_s)
    arrive(wbuf.at[pl.ds(0, 3), :, :, 0], p2_s)
    arrive(wbuf.at[:, :, :, 0], c_s)
    arrive(rsb, rs_s)
    arrive(xsend, xp_s)
    arrive(wf.at[0, :, pl.ds(0, 7 * 128)], ag_s.at[0])
    arrive(wf.at[0, :, pl.ds(0, 8 * 128)], ag_s.at[1])
    arrive(wf.at[0], cc_s)
    arrive(rbuf.at[0, pl.ds(0, 7)], r_s.at[0])
    arrive(rbuf.at[0], r_s.at[1])
    for i, buf in enumerate((a1, b1, a2, b2)):
        arrive(buf.at[pl.ds(0, 3)], e_s.at[i])


def combine(caps, ids_ref, gates_ref, tot_ref, proj_ref, out_ref, sum_ref):
    out_ref[...] = proj_ref[...]
    firsts, seconds, rows = [], [], []
    for e in range(2):
        gate = jnp.zeros((1, TOK), F32)
        for i in range(PICKS):
            gate += jnp.where(ids_ref[i] == e, gates_ref[i], 0.0)
        high = gate.astype(BF).astype(F32)
        first, second = slot_rows(ids_ref, caps[e], e)
        for g in (high, gate - high):
            firsts.append(first * g)
            seconds.append(second * g)
            rows.append(tot_ref[e])
    rows = jnp.concatenate(rows, axis=0)
    sum_ref[:, :1024] = dot(jnp.concatenate(firsts, axis=0).astype(BF), rows, TN).astype(BF)
    sum_ref[:, 1024:] = dot(jnp.concatenate(seconds, axis=0).astype(BF), rows, TN).astype(BF)


def body(
    query_vecs, key_vecs, value_vecs, residual, w_out, norm_gain, w_gate_up,
    w_down, expert_ids, route_gates, capacity, expert_owner,
):
    hbm = pl.BlockSpec(memory_space=pl.ANY)
    vmem = pl.BlockSpec(memory_space=pltpu.VMEM)
    smem = pl.BlockSpec(memory_space=pltpu.SMEM)
    dma = pltpu.SemaphoreType.DMA
    out = jax.ShapeDtypeStruct((TOK, D), BF)
    rows = (2 * CAP, 1024)
    half = (2 * CAP, 512)
    ids = jnp.transpose(expert_ids, (2, 0, 1))
    gates = jnp.transpose(route_gates, (2, 0, 1))
    proj, tot = pl.pallas_call(
        kernel,
        out_shape=(out, jax.ShapeDtypeStruct((2,) + rows, BF)),
        in_specs=[smem, smem] + [hbm] * 7 + [vmem] * 2,
        out_specs=(vmem, vmem),
        scratch_shapes=[
            pltpu.VMEM((3, NCTX, TOK, HD), BF),
            pltpu.VMEM((NCTX, TOK, HD), BF),
            pltpu.VMEM((TOK, NCTX * HD), BF),
            pltpu.VMEM((NX, NY, NZ, 2, 16, 256), BF),
            pltpu.VMEM((TOK, D), BF),
            pltpu.VMEM((3 * FF_DEV, D), BF),
            pltpu.VMEM((2, HALF, 128), BF),
            pltpu.VMEM((2, 2, HALF, 128), BF),
            pltpu.VMEM((HALF, D), BF),
            pltpu.VMEM((2, NZ, HALF, 128), BF),
            pltpu.VMEM((2, NZ - 1, HALF, 128), BF),
            pltpu.VMEM((HALF, 128), BF),
            pltpu.VMEM((HALF, 128), BF),
            pltpu.VMEM((2, HALF, D), BF),
            pltpu.VMEM((FF_DEV, D), BF),
            pltpu.VMEM((TOK, D), BF),
            pltpu.VMEM((2, NCTX) + rows, BF),
            pltpu.VMEM(rows, BF),
            pltpu.VMEM((2, NX, NY) + half, BF),
            pltpu.VMEM((NY, NX) + half, BF),
            pltpu.VMEM((NX, NY) + half, BF),
            pltpu.VMEM((NX,) + half, BF),
            pltpu.VMEM((NY, 2) + half, BF),
            pltpu.VMEM((NX,) + half, BF),
            pltpu.VMEM((NY, 2) + half, BF),
            dma, dma((NCTX,)), dma, dma, dma((2,)), dma((2,)),
            dma, dma((2,)), dma, dma((2, 4)), dma, dma,
            dma((2,)), dma, dma, dma, dma, dma, dma((2, NZ - 1, 2)), dma, dma,
            dma((2,)), dma((2, HOPS)), dma, dma,
            dma((2,)), dma((2,)), dma((4,)), dma((4,)),
        ],
        compiler_params=pltpu.CompilerParams(
            collective_id=0, has_side_effects=True, vmem_limit_bytes=58 << 20
        ),
    )(
        expert_owner[:2], capacity[0, 0],
        query_vecs[0], key_vecs[0], value_vecs[0], residual[0], w_out,
        jnp.swapaxes(w_gate_up[0], 1, 2), w_down[0], norm_gain[None], ids,
    )
    attn_proj, expert_sum = pl.pallas_call(
        combine,
        out_shape=(out, out),
        in_specs=[smem] + [vmem] * 4,
        out_specs=(vmem, vmem),
    )(capacity[0, 0], ids, gates, tot, proj)
    return (attn_proj[None], expert_sum[None])


def solution(mesh):
    seq = P("dp", "ctx", None)
    placed = (
        seq, seq, seq, seq, P("dp", None), P(),
        P("dp", None, None, "ctx"), seq, seq, seq, seq, P(),
    )
    return jax.shard_map(
        body, mesh=mesh, in_specs=placed, out_specs=(seq, seq), check_vma=False
    )
```
